512 devices in a mesh: doc: 16 (over y_lo, x, core), blk: 32 (over y_hi, z).
Axes of the slice: x: 4, y: 4 (y_hi: 2, y_lo: 2; y = y_hi * 2 + y_lo), z: 16, core: 2. Of those that a mesh axis runs over, the one named last changes fastest.
Arguments:
- query_rows: bfloat16 [256, 98304], P('blk', 'doc'), may hold values from -6 to 6
- row_values: bfloat16 [16, 32, 32, 128, 256], P('doc', 'blk'), may hold values from -0.25 to 0.25
- row_slots: int32 [16, 32, 32, 128], P('doc', 'blk'), may hold values from 0 to 49151, as said below
- row_counts: int32 [16, 32, 32], P('doc', 'blk'), may hold values from 16 to 128, as said below
Outputs:
- gram: float32 [256, 65536], P('doc', 'blk')
The draws below stay inside these ranges and needn't reach their ends.
Inputs may be any that keep to these rules, and one draw needn't show every extreme that they name: row_slots[d, s, o, j] = (s * 192 + e) * 8 + b for a document e of source s's 192 and a feature block b of owner o; the 128 entries of one (d, s, o) are distinct. Slots j >= row_counts[d, s, o] carry no data; for every d some owner receives 128 rows from every source.
All inputs are finite; a program needn't handle non-finite values.
Results may differ from the reference program's by a relative error of at most 0.0003.
Values may be sent and summed in bfloat16 or wider, within the bound.
No kernel may reach another device: no remote copies, remote signals or barrier semaphores. Data moves between devices by JAX's collectives and lax.ppermute only.
A program may use at most 192 MiB of HBM per device.

```python
import jax
import jax.numpy as jnp
from jax import lax

F = 65536
BW = 256
DOC_DEV = 192
C_OWN = 2048
BPO = 8
DOCS = 6144
NDOCS = 98304
NQ = 256
CAP = 128
N_DOC = 16
N_BLK = 32


def draw_row_slots(key, part):
    span = DOC_DEV * BPO
    key_list = jax.random.split(jax.random.fold_in(key, 11), N_DOC * N_BLK * N_BLK)
    picked = jax.vmap(lambda single: jax.random.permutation(single, span)[:CAP])(key_list)
    picked = picked.reshape(N_DOC, N_BLK, N_BLK, CAP).astype(jnp.int32)
    offset = (jnp.arange(N_BLK, dtype=jnp.int32) * span)[None, :, None, None]
    return picked + offset


def draw_row_counts(key, part):
    drawn_counts = jax.random.randint(jax.random.fold_in(key, 23), (N_DOC, N_BLK, N_BLK), CAP // 8, 3 * CAP // 4 + 1)
    hot_owner = jax.random.randint(jax.random.fold_in(key, 29), (N_DOC,), 0, N_BLK)
    is_hot = jnp.arange(N_BLK)[None, None, :] == hot_owner[:, None, None]
    return jnp.where(is_hot, CAP, drawn_counts).astype(jnp.int32)


def block_scale(key, shape, shards, least, top_value):
    level, own = 1.0, jax.random.fold_in(key, 6)
    for dim, blocks in shards:
        draws = jnp.exp(jax.random.uniform(jax.random.fold_in(own, dim), (blocks,), jnp.float32, least / len(shards), top_value / len(shards)))
        level = level * jnp.repeat(draws, shape[dim] // blocks).reshape([-1 if axis == dim else 1 for axis in range(len(shape))])
    return level


def noise(own_key, dims, spread, limit, cuts=(), kind=jnp.bfloat16):
    loudness = block_scale(own_key, dims, cuts, -0.22, 0.18) if cuts else 1.0
    values = jax.random.normal(own_key, dims, jnp.float32) * spread * loudness
    return jnp.minimum(jnp.maximum(values, -limit), limit).astype(kind)


def setup_inputs(seed: int = 0) -> dict:
    splits = jax.random.split(jax.random.key(seed), 5)
    return {
        "query_rows": noise(splits[0], (NQ, NDOCS), 1.0, 6.0, ((0, 32), (1, 16))),
        "row_values": noise(splits[1], (N_DOC, N_BLK, N_BLK, CAP, BW), ((3.0 * BPO / NDOCS) ** 0.5), 0.25, ((0, 16), (1, 32))),
        "row_slots": draw_row_slots(jax.random.fold_in(splits[4], 71), 0),
        "row_counts": draw_row_counts(jax.random.fold_in(splits[4], 71), 0),
    }


def build_panel(values, slot_ids, counts):
    live_slot = jnp.arange(CAP, dtype=jnp.int32)[None, :] < counts[:, None]
    slot_index = jnp.where(live_slot, slot_ids, DOCS * BPO).reshape(-1).astype(jnp.int32)
    dense_panel = jnp.zeros((DOCS * BPO, BW), jnp.bfloat16)
    dense_panel = dense_panel.at[slot_index].set(values.reshape(-1, BW), mode="drop")
    return dense_panel.reshape(DOCS, C_OWN)


def reference(query_rows, row_values, row_slots, row_counts):
    def add_group(group_index, running):
        start = (group_index * DOCS).astype(jnp.int32)
        queries = lax.dynamic_slice_in_dim(query_rows, start, DOCS, 1)
        group_values = lax.dynamic_index_in_dim(row_values, group_index, 0, keepdims=False)
        group_slots = lax.dynamic_index_in_dim(row_slots, group_index, 0, keepdims=False)
        group_counts = lax.dynamic_index_in_dim(row_counts, group_index, 0, keepdims=False)

        def owner_tile(owner):
            dense_panel = build_panel(group_values[:, owner], group_slots[:, owner], group_counts[:, owner])
            return jnp.dot(queries, dense_panel, preferred_element_type=jnp.float32)

        owner_tiles = lax.map(owner_tile, jnp.arange(N_BLK, dtype=jnp.int32))
        return running + owner_tiles.transpose(1, 0, 2).reshape(NQ, F)

    return lax.fori_loop(0, N_DOC, add_group, jnp.zeros((NQ, F), jnp.float32))
```

```python
import functools

import jax
import jax.numpy as jnp
from jax import lax
from jax.experimental import pallas as pl
from jax.experimental.pallas import tpu as pltpu
from jax.sharding import PartitionSpec as P

Y_PARTS = 2
CODE_STEP = 64.0
TOP = 32700.0
TINY = 2.0**-110
LANES = 128


def gram_kernel(flip_ref, q_ref, x_ref, o_ref, left, acc, *, cap, span, per_step, blocks):
    step = pl.program_id(0)
    width = x_ref.shape[2]
    nq = q_ref.shape[0]
    pair_rows = 2 * cap
    for pair in range(per_step // 2):
        docs, ids = [], []
        for k in range(2):
            meta = x_ref[2 * pair + k, cap : cap + 8, :][0:1, :].astype(jnp.float32)
            docs.append(meta[:, :cap] + float(k * span))
            ids.append(meta[:, cap : 2 * cap])
        doc = jnp.concatenate(docs, axis=1).astype(jnp.int32)
        block = jnp.concatenate(ids, axis=1)
        rows = lax.broadcasted_iota(jnp.int32, (2 * span, pair_rows), 0)
        chosen = jnp.where(rows == doc, 1.0, 0.0).astype(jnp.bfloat16)
        queries = q_ref[:, pair * 2 * span : (pair + 1) * 2 * span]
        picked = jnp.dot(queries, chosen, preferred_element_type=jnp.float32)
        for b in range(blocks):
            kept = jnp.where(block == float(b), picked, 0.0).astype(jnp.bfloat16)
            left[b * nq : (b + 1) * nq, pair * pair_rows : (pair + 1) * pair_rows] = kept
    right = jnp.concatenate([x_ref[k, :cap, :] for k in range(per_step)], axis=0)
    product = jnp.dot(left[...], right, preferred_element_type=jnp.float32)

    @pl.when(step == 0)
    def _():
        acc[...] = product

    @pl.when(step > 0)
    def _():
        acc[...] += product

    @pl.when(step == pl.num_programs(0) - 1)
    def _():
        flip = flip_ref[0]
        half = nq // (2 * 16)
        lane = lax.broadcasted_iota(jnp.int32, (16, LANES), 1)
        for m in range(half):
            for slot in range(2):
                target = (slot + flip - 2 * slot * flip) * half + m
                codes = jnp.zeros((16, LANES), jnp.int32)
                for b in range(blocks):
                    base = b * nq + m * 32 + slot * 8
                    tile = jnp.concatenate([acc[base : base + 8, :], acc[base + 16 : base + 24, :]], axis=0)
                    peak = jnp.maximum(jnp.max(jnp.abs(tile), axis=1, keepdims=True), TINY)
                    code = jnp.ceil((jnp.log2(peak) - jnp.log2(TOP)) * CODE_STEP)
                    coded = tile * jnp.exp2(code * (-1.0 / CODE_STEP))
                    coded = jnp.floor(coded + 0.5).astype(jnp.int32).astype(jnp.int16)
                    o_ref[target, :, b * width : (b + 1) * width] = coded
                    codes = jnp.where(lane == b, code.astype(jnp.int32), codes)
                o_ref[target, :, blocks * width :] = codes.astype(jnp.int16)


def partial_tile(flip, queries, rows, *, cap, span, blocks, per_step=8):
    nq, docs = queries.shape
    sources, _, width = rows.shape
    lanes = blocks * width + LANES
    grid_spec = pltpu.PrefetchScalarGridSpec(
        num_scalar_prefetch=1,
        grid=(sources // per_step,),
        in_specs=[
            pl.BlockSpec((nq, per_step * span), lambda i, _: (0, i)),
            pl.BlockSpec((per_step, rows.shape[1], width), lambda i, _: (i, 0, 0)),
        ],
        out_specs=pl.BlockSpec((16, nq // 16, lanes), lambda i, _: (0, 0, 0)),
        scratch_shapes=[
            pltpu.VMEM((blocks * nq, per_step * cap), jnp.bfloat16),
            pltpu.VMEM((blocks * nq, width), jnp.float32),
        ],
    )
    return pl.pallas_call(
        functools.partial(gram_kernel, cap=cap, span=span, per_step=per_step, blocks=blocks),
        grid_spec=grid_spec,
        out_shape=jax.ShapeDtypeStruct((16, nq // 16, lanes), jnp.int16),
        compiler_params=pltpu.CompilerParams(vmem_limit_bytes=48 << 20),
        cost_estimate=pl.CostEstimate(
            flops=2 * nq * sources * cap * width * blocks,
            bytes_accessed=2 * (queries.size + rows.size),
            transcendentals=0,
        ),
        name="gram_tile",
    )(flip, queries, rows)


def sum_kernel(p_ref, o_ref, *, blocks, width):
    groups = p_ref.shape[0]
    scale = jnp.exp2(p_ref[:, :, blocks * width :].astype(jnp.float32) * (1.0 / CODE_STEP))
    for b in range(blocks):
        total = jnp.zeros((p_ref.shape[1], width), jnp.float32)
        for g in range(groups):
            part = p_ref[g, :, b * width : (b + 1) * width].astype(jnp.float32)
            total = total + part * scale[g, :, b : b + 1]
        o_ref[:, b * width : (b + 1) * width] = total


def summed(parts, *, blocks, width):
    return pl.pallas_call(
        functools.partial(sum_kernel, blocks=blocks, width=width),
        out_shape=jax.ShapeDtypeStruct((parts.shape[1], blocks * width), jnp.float32),
        in_specs=[pl.BlockSpec(memory_space=pltpu.VMEM)],
        out_specs=pl.BlockSpec(memory_space=pltpu.VMEM),
        compiler_params=pltpu.CompilerParams(vmem_limit_bytes=16 << 20),
        name="sum_parts",
    )(parts)


def per_device(query_rows, row_values, row_slots, row_counts):
    owners = lax.axis_size("blk")
    z_size = owners // Y_PARTS
    doc_count = query_rows.shape[1]
    span = doc_count // owners
    _, _, _, cap, width = row_values.shape
    blocks = 8
    me = lax.axis_index("blk")

    across = [(i, (i + z_size) % owners) for i in range(owners)]
    mirror = lax.ppermute(query_rows, "blk", across)
    both = jnp.concatenate([query_rows, mirror], axis=0)
    rings = [list(range(h * z_size, (h + 1) * z_size)) for h in range(Y_PARTS)]
    queries = lax.all_gather(both, "blk", axis=0, tiled=True, axis_index_groups=rings)

    slots = row_slots[0, 0]
    live = jnp.arange(cap, dtype=jnp.int32)[None, :] < row_counts[0, 0][:, None]
    doc = (slots // blocks - me * span).astype(jnp.bfloat16)
    block = jnp.where(live, slots % blocks, 2 * blocks).astype(jnp.bfloat16)
    meta = jnp.concatenate([doc, block], axis=1)[:, None, :]
    meta = jnp.pad(meta, ((0, 0), (0, 7), (0, 0)))
    sent = jnp.concatenate([row_values[0, 0], meta], axis=1)
    rows = lax.all_to_all(sent, "blk", split_axis=0, concat_axis=0, tiled=True)

    flip = (me // z_size).astype(jnp.int32).reshape(1)
    coded = partial_tile(flip, queries, rows, cap=cap, span=span, blocks=blocks)
    parts = lax.all_to_all(coded, "doc", split_axis=0, concat_axis=0, tiled=True)
    return summed(parts, blocks=blocks, width=width)


def solution(mesh):
    in_specs = (
        P("blk", "doc"),
        P("doc", "blk", None, None, None),
        P("doc", "blk", None, None),
        P("doc", "blk", None),
    )
    out_specs = P("doc", "blk")
    return jax.shard_map(
        per_device, mesh=mesh, in_specs=in_specs, out_specs=out_specs, check_vma=False
    )
```

```python
import functools

import jax
import jax.numpy as jnp
from jax import lax
from jax.experimental import pallas as pl
from jax.experimental.pallas import tpu as pltpu
from jax.sharding import PartitionSpec as P

Y_PARTS = 2
CODE_STEP = 64.0
TOP = 32700.0
TINY = 2.0**-110
LANES = 128


def gram_kernel(flip_ref, q_ref, x_ref, o_ref, left, acc, *, cap, span, per_step, blocks):
    step = pl.program_id(0)
    width = x_ref.shape[2]
    nq = q_ref.shape[0]
    pair_rows = 2 * cap
    for pair in range(per_step // 2):
        docs, ids = [], []
        for k in range(2):
            meta = x_ref[2 * pair + k, cap : cap + 8, :][0:1, :].astype(jnp.float32)
            docs.append(meta[:, :cap] + float(k * span))
            ids.append(meta[:, cap : 2 * cap])
        doc = jnp.concatenate(docs, axis=1).astype(jnp.int32)
        block = jnp.concatenate(ids, axis=1)
        rows = lax.broadcasted_iota(jnp.int32, (2 * span, pair_rows), 0)
        chosen = jnp.where(rows == doc, 1.0, 0.0).astype(jnp.bfloat16)
        queries = q_ref[:, pair * 2 * span : (pair + 1) * 2 * span]
        picked = jnp.dot(queries, chosen, preferred_element_type=jnp.float32).astype(jnp.bfloat16)
        for b in range(blocks):
            kept = picked * jnp.where(block == float(b), 1.0, 0.0).astype(jnp.bfloat16)
            left[b * nq : (b + 1) * nq, pair * pair_rows : (pair + 1) * pair_rows] = kept
    right = jnp.concatenate([x_ref[k, :cap, :] for k in range(per_step)], axis=0)
    product = jnp.dot(left[...], right, preferred_element_type=jnp.float32)

    @pl.when(step == 0)
    def _():
        acc[...] = product

    @pl.when(step > 0)
    def _():
        acc[...] += product

    @pl.when(step == pl.num_programs(0) - 1)
    def _():
        flip = flip_ref[0]
        half = nq // (2 * 16)
        lane = lax.broadcasted_iota(jnp.int32, (16, LANES), 1)
        for m in range(half):
            for slot in range(2):
                target = (slot + flip - 2 * slot * flip) * half + m
                codes = jnp.zeros((16, LANES), jnp.int32)
                for b in range(blocks):
                    base = b * nq + m * 32 + slot * 8
                    tile = jnp.concatenate([acc[base : base + 8, :], acc[base + 16 : base + 24, :]], axis=0)
                    peak = jnp.maximum(jnp.max(jnp.abs(tile), axis=1, keepdims=True), TINY)
                    code = jnp.ceil((jnp.log2(peak) - jnp.log2(TOP)) * CODE_STEP)
                    coded = tile * jnp.exp2(code * (-1.0 / CODE_STEP))
                    coded = jnp.floor(coded + 0.5).astype(jnp.int32).astype(jnp.int16)
                    o_ref[target, :, b * width : (b + 1) * width] = coded
                    codes = jnp.where(lane == b, code.astype(jnp.int32), codes)
                o_ref[target, :, blocks * width :] = codes.astype(jnp.int16)


def partial_tile(flip, queries, rows, *, cap, span, blocks, per_step=8):
    nq, docs = queries.shape
    sources, _, width = rows.shape
    lanes = blocks * width + LANES
    grid_spec = pltpu.PrefetchScalarGridSpec(
        num_scalar_prefetch=1,
        grid=(sources // per_step,),
        in_specs=[
            pl.BlockSpec((nq, per_step * span), lambda i, _: (0, i)),
            pl.BlockSpec((per_step, rows.shape[1], width), lambda i, _: (i, 0, 0)),
        ],
        out_specs=pl.BlockSpec((16, nq // 16, lanes), lambda i, _: (0, 0, 0)),
        scratch_shapes=[
            pltpu.VMEM((blocks * nq, per_step * cap), jnp.bfloat16),
            pltpu.VMEM((blocks * nq, width), jnp.float32),
        ],
    )
    return pl.pallas_call(
        functools.partial(gram_kernel, cap=cap, span=span, per_step=per_step, blocks=blocks),
        grid_spec=grid_spec,
        out_shape=jax.ShapeDtypeStruct((16, nq // 16, lanes), jnp.int16),
        compiler_params=pltpu.CompilerParams(vmem_limit_bytes=48 << 20),
        cost_estimate=pl.CostEstimate(
            flops=2 * nq * sources * cap * width * blocks,
            bytes_accessed=2 * (queries.size + rows.size),
            transcendentals=0,
        ),
        name="gram_tile",
    )(flip, queries, rows)


def held_kernel(q_ref, o_ref):
    pltpu.touch(o_ref)


def held(queries):
    return pl.pallas_call(
        held_kernel,
        out_shape=jax.ShapeDtypeStruct(queries.shape, queries.dtype),
        in_specs=[pl.BlockSpec(memory_space=pl.ANY)],
        out_specs=pl.BlockSpec(memory_space=pl.ANY),
        input_output_aliases={0: 0},
        cost_estimate=pl.CostEstimate(flops=10**12, bytes_accessed=10**6, transcendentals=0),
        name="held",
    )(queries)


def sum_kernel(p_ref, o_ref, *, blocks, width):
    groups = p_ref.shape[0]
    scale = jnp.exp2(p_ref[:, :, blocks * width :].astype(jnp.float32) * (1.0 / CODE_STEP))
    for b in range(blocks):
        total = jnp.zeros((p_ref.shape[1], width), jnp.float32)
        for g in range(groups):
            part = p_ref[g, :, b * width : (b + 1) * width].astype(jnp.float32)
            total = total + part * scale[g, :, b : b + 1]
        o_ref[:, b * width : (b + 1) * width] = total


def summed(parts, *, blocks, width):
    return pl.pallas_call(
        functools.partial(sum_kernel, blocks=blocks, width=width),
        out_shape=jax.ShapeDtypeStruct((parts.shape[1], blocks * width), jnp.float32),
        in_specs=[pl.BlockSpec(memory_space=pltpu.VMEM)],
        out_specs=pl.BlockSpec(memory_space=pltpu.VMEM),
        compiler_params=pltpu.CompilerParams(vmem_limit_bytes=16 << 20),
        name="sum_parts",
    )(parts)


def per_device(query_rows, row_values, row_slots, row_counts):
    owners = lax.axis_size("blk")
    z_size = owners // Y_PARTS
    doc_count = query_rows.shape[1]
    span = doc_count // owners
    _, _, _, cap, width = row_values.shape
    blocks = 8
    me = lax.axis_index("blk")

    across = [(i, (i + z_size) % owners) for i in range(owners)]
    mirror = lax.ppermute(query_rows, "blk", across)
    both = jnp.concatenate([query_rows, mirror], axis=0)
    rings = [list(range(h * z_size, (h + 1) * z_size)) for h in range(Y_PARTS)]
    slots = row_slots[0, 0]
    live = jnp.arange(cap, dtype=jnp.int32)[None, :] < row_counts[0, 0][:, None]
    doc = (slots // blocks - me * span).astype(jnp.bfloat16)
    block = jnp.where(live, slots % blocks, 2 * blocks).astype(jnp.bfloat16)
    meta = jnp.concatenate([doc, block], axis=1)[:, None, :]
    meta = jnp.pad(meta, ((0, 0), (0, 7), (0, 0)))
    values, both = lax.optimization_barrier((row_values[0, 0], both))
    sent = jnp.concatenate([values, meta], axis=1)
    queries = lax.all_gather(both, "blk", axis=0, tiled=True, axis_index_groups=rings)
    rows = lax.all_to_all(sent, "blk", split_axis=0, concat_axis=0, tiled=True)

    flip = (me // z_size).astype(jnp.int32).reshape(1)
    coded = partial_tile(flip, held(queries), rows, cap=cap, span=span, blocks=blocks)
    parts = lax.all_to_all(coded, "doc", split_axis=0, concat_axis=0, tiled=True)
    return summed(parts, blocks=blocks, width=width)


def solution(mesh):
    in_specs = (
        P("blk", "doc"),
        P("doc", "blk", None, None, None),
        P("doc", "blk", None, None),
        P("doc", "blk", None),
    )
    out_specs = P("doc", "blk")
    return jax.shard_map(
        per_device, mesh=mesh, in_specs=in_specs, out_specs=out_specs, check_vma=False
    )
```

```python
import functools

import jax
import jax.numpy as jnp
from jax import lax
from jax.experimental import pallas as pl
from jax.experimental.pallas import tpu as pltpu
from jax.sharding import Mesh
from jax.sharding import PartitionSpec as P

HALVES = 2
CODE_STEP = 64.0
TOP = 32700.0
TINY = 2.0**-110
LANES = 128
TILE = 8


def gram_kernel(flip_ref, q_ref, x_ref, o_ref, left, acc, *, cap, span, per_step, blocks):
    step = pl.program_id(0)
    width = x_ref.shape[2]
    nq = q_ref.shape[0]
    pair_rows = 2 * cap
    for owner in range(HALVES):
        for pair in range(per_step // 2):
            docs, ids = [], []
            for k in range(2):
                base = HALVES * cap
                meta = x_ref[2 * pair + k, base : base + TILE, :][owner : owner + 1, :].astype(jnp.float32)
                docs.append(meta[:, :cap] + float(k * span))
                ids.append(meta[:, cap : 2 * cap])
            doc = jnp.concatenate(docs, axis=1).astype(jnp.int32)
            block = jnp.concatenate(ids, axis=1)
            rows = lax.broadcasted_iota(jnp.int32, (2 * span, pair_rows), 0)
            chosen = jnp.where(rows == doc, 1.0, 0.0).astype(jnp.bfloat16)
            queries = q_ref[:, pair * 2 * span : (pair + 1) * 2 * span]
            picked = jnp.dot(queries, chosen, preferred_element_type=jnp.float32).astype(jnp.bfloat16)
            for b in range(blocks):
                kept = picked * jnp.where(block == float(b), 1.0, 0.0).astype(jnp.bfloat16)
                left[owner, b * nq : (b + 1) * nq, pair * pair_rows : (pair + 1) * pair_rows] = kept
        right = jnp.concatenate([x_ref[k, owner * cap : (owner + 1) * cap, :] for k in range(per_step)], axis=0)
        product = jnp.dot(left[owner], right, preferred_element_type=jnp.float32)

        @pl.when(step == 0)
        def _():
            acc[owner] = product

        @pl.when(step > 0)
        def _():
            acc[owner] += product

    @pl.when(step == pl.num_programs(0) - 1)
    def _():
        flip = flip_ref[0]
        half = nq // (2 * 16)
        lane = lax.broadcasted_iota(jnp.int32, (16, LANES), 1)
        for owner in range(HALVES):
            for m in range(half):
                for slot in range(2):
                    target = ((slot + flip - 2 * slot * flip) * half + m) * HALVES + owner
                    codes = jnp.zeros((16, LANES), jnp.int32)
                    for b in range(blocks):
                        base = b * nq + m * 32 + slot * 8
                        tile = jnp.concatenate([acc[owner, base : base + 8, :], acc[owner, base + 16 : base + 24, :]], axis=0)
                        peak = jnp.maximum(jnp.max(jnp.abs(tile), axis=1, keepdims=True), TINY)
                        code = jnp.ceil((jnp.log2(peak) - jnp.log2(TOP)) * CODE_STEP)
                        coded = tile * jnp.exp2(code * (-1.0 / CODE_STEP))
                        coded = jnp.floor(coded + 0.5).astype(jnp.int32).astype(jnp.int16)
                        o_ref[target, :, b * width : (b + 1) * width] = coded
                        codes = jnp.where(lane == b, code.astype(jnp.int32), codes)
                    o_ref[target, :, blocks * width :] = codes.astype(jnp.int16)


def partial_tiles(flip, queries, rows, *, cap, span, blocks, per_step=4):
    nq, docs = queries.shape
    sources, depth, width = rows.shape
    lanes = blocks * width + LANES
    targets = 16 * HALVES
    grid_spec = pltpu.PrefetchScalarGridSpec(
        num_scalar_prefetch=1,
        grid=(sources // per_step,),
        in_specs=[
            pl.BlockSpec((nq, per_step * span), lambda i, _: (0, i)),
            pl.BlockSpec((per_step, depth, width), lambda i, _: (i, 0, 0)),
        ],
        out_specs=pl.BlockSpec((targets, nq // 16, lanes), lambda i, _: (0, 0, 0)),
        scratch_shapes=[
            pltpu.VMEM((HALVES, blocks * nq, per_step * cap), jnp.bfloat16),
            pltpu.VMEM((HALVES, blocks * nq, width), jnp.float32),
        ],
    )
    return pl.pallas_call(
        functools.partial(gram_kernel, cap=cap, span=span, per_step=per_step, blocks=blocks),
        grid_spec=grid_spec,
        out_shape=jax.ShapeDtypeStruct((targets, nq // 16, lanes), jnp.int16),
        compiler_params=pltpu.CompilerParams(vmem_limit_bytes=48 << 20),
        cost_estimate=pl.CostEstimate(
            flops=2 * nq * sources * HALVES * cap * width * blocks,
            bytes_accessed=2 * (queries.size + rows.size),
            transcendentals=0,
        ),
        name="gram_tiles",
    )(flip, queries, rows)


def held_kernel(q_ref, o_ref):
    pltpu.touch(o_ref)


def held(queries):
    return pl.pallas_call(
        held_kernel,
        out_shape=jax.ShapeDtypeStruct(queries.shape, queries.dtype),
        in_specs=[pl.BlockSpec(memory_space=pl.ANY)],
        out_specs=pl.BlockSpec(memory_space=pl.ANY),
        input_output_aliases={0: 0},
        cost_estimate=pl.CostEstimate(flops=10**12, bytes_accessed=10**6, transcendentals=0),
        name="held",
    )(queries)


def sum_kernel(p_ref, o_ref, *, blocks, width):
    groups = p_ref.shape[0]
    scale = jnp.exp2(p_ref[:, :, blocks * width :].astype(jnp.float32) * (1.0 / CODE_STEP))
    for b in range(blocks):
        total = jnp.zeros((p_ref.shape[1], width), jnp.float32)
        for g in range(groups):
            part = p_ref[g, :, b * width : (b + 1) * width].astype(jnp.float32)
            total = total + part * scale[g, :, b : b + 1]
        o_ref[:, b * width : (b + 1) * width] = total


def summed(parts, *, blocks, width):
    return pl.pallas_call(
        functools.partial(sum_kernel, blocks=blocks, width=width),
        out_shape=jax.ShapeDtypeStruct((parts.shape[1], blocks * width), jnp.float32),
        in_specs=[pl.BlockSpec(memory_space=pltpu.VMEM)],
        out_specs=pl.BlockSpec(memory_space=pltpu.VMEM),
        compiler_params=pltpu.CompilerParams(vmem_limit_bytes=16 << 20),
        name="sum_parts",
    )(parts)


def per_device(query_rows, row_values, row_slots, row_counts):
    z_size = lax.axis_size("z")
    owners = HALVES * z_size
    doc_count = query_rows.shape[1]
    span = doc_count // owners
    _, _, _, cap, width = row_values.shape
    blocks = 8
    y = lax.axis_index("y")
    me = y * z_size + lax.axis_index("z")

    half_docs = doc_count // HALVES
    mine = lax.dynamic_slice_in_dim(query_rows, y * half_docs, half_docs, 1)
    theirs = lax.dynamic_slice_in_dim(query_rows, (1 - y) * half_docs, half_docs, 1)
    mirror = lax.ppermute(theirs, "y", [(0, 1), (1, 0)])
    both = jnp.concatenate([mine, mirror], axis=0)

    slots = row_slots[0, 0]
    live = jnp.arange(cap, dtype=jnp.int32)[None, :] < row_counts[0, 0][:, None]
    doc = (slots // blocks - me * span).astype(jnp.bfloat16)
    block = jnp.where(live, slots % blocks, 2 * blocks).astype(jnp.bfloat16)
    meta = jnp.concatenate([doc, block], axis=1).reshape(HALVES, z_size, 2 * cap).transpose(1, 0, 2)
    meta = jnp.pad(meta, ((0, 0), (0, TILE - HALVES), (0, 0)))
    values, both = lax.optimization_barrier((row_values[0, 0], both))
    sent = jnp.concatenate([values[:z_size], values[z_size:], meta], axis=1)

    queries = lax.all_gather(both, "z", axis=0, tiled=True)
    rows = lax.all_to_all(sent, "z", split_axis=0, concat_axis=0, tiled=True)

    coded = partial_tiles(y.astype(jnp.int32).reshape(1), held(queries), rows, cap=cap, span=span, blocks=blocks)
    parts = lax.all_to_all(coded, ("doc", "y"), split_axis=0, concat_axis=0, tiled=True)
    return summed(parts, blocks=blocks, width=width)


def solution(mesh):
    docs, owners = mesh.devices.shape
    split = Mesh(mesh.devices.reshape(docs, HALVES, owners // HALVES), ("doc", "y", "z"))
    blk = ("y", "z")
    in_specs = (
        P(blk, "doc"),
        P("doc", blk, None, None, None),
        P("doc", blk, None, None),
        P("doc", blk, None),
    )
    return jax.shard_map(
        per_device, mesh=split, in_specs=in_specs, out_specs=P("doc", blk), check_vma=False
    )
```

```python
import functools

import jax
import jax.numpy as jnp
from jax import lax
from jax.experimental import pallas as pl
from jax.experimental.pallas import tpu as pltpu
from jax.sharding import Mesh
from jax.sharding import PartitionSpec as P

HALVES = 2
CODE_STEP = 64.0
TOP = 32700.0
TINY = 2.0**-110
LANES = 128
TILE = 8
SHALLOW = 96
EXTRA = 48
DEAD = 64


def code_tiles(flip_ref, acc, o_ref, *, nq, blocks):
    width = acc.shape[2]
    flip = flip_ref[0]
    half = nq // (2 * 16)
    lane = lax.broadcasted_iota(jnp.int32, (16, LANES), 1)

    def tile_of(owner, b, m, slot):
        base = b * nq + m * 32 + slot * 8
        return jnp.concatenate([acc[owner, base : base + 8, :], acc[owner, base + 16 : base + 24, :]], axis=0)

    for owner in range(HALVES):
        for m in range(half):
            for slot in range(2):
                target = ((slot + flip - 2 * slot * flip) * half + m) * HALVES + owner
                peaks = jnp.full((16, LANES), TINY, jnp.float32)
                for b in range(blocks):
                    peak = jnp.max(jnp.abs(tile_of(owner, b, m, slot)), axis=1, keepdims=True)
                    peaks = jnp.where(lane == b, jnp.maximum(peak, TINY), peaks)
                code = jnp.ceil((jnp.log2(peaks) - jnp.log2(TOP)) * CODE_STEP)
                inverse = jnp.exp2(code * (-1.0 / CODE_STEP))
                for b in range(blocks):
                    coded = tile_of(owner, b, m, slot) * inverse[:, b : b + 1]
                    coded = jnp.floor(coded + 0.5).astype(jnp.int32).astype(jnp.int16)
                    o_ref[target, :, b * width : (b + 1) * width] = coded
                o_ref[target, :, blocks * width :] = code.astype(jnp.int32).astype(jnp.int16)


def lean_kernel(flip_ref, q_ref, deep_ref, x_ref, o_ref, left, acc, *, cap, span, per_step, blocks, extra):
    step = pl.program_id(0)
    width = x_ref.shape[2]
    nq = q_ref.shape[0]
    base = HALVES * cap
    group = 4

    def chosen(doc, docs):
        rows = lax.broadcasted_iota(jnp.int32, (docs, doc.shape[1]), 0)
        return jnp.where(rows == doc.astype(jnp.int32), 1.0, 0.0).astype(jnp.bfloat16)

    def picked(doc, first, count):
        queries = q_ref[:, first * span : (first + count) * span]
        return jnp.dot(queries, chosen(doc, count * span), preferred_element_type=jnp.float32).astype(jnp.bfloat16)

    metas = [x_ref[k, base : base + TILE, :].astype(jnp.float32) for k in range(per_step)]
    deep_doc = jnp.concatenate([metas[k][2:3, :extra] + float(k * span) for k in range(per_step)], axis=1)
    deep_block = jnp.concatenate([metas[k][2:3, LANES : LANES + extra] for k in range(per_step)], axis=1)
    deep_picked = picked(deep_doc, 0, per_step)
    deep_rows = [deep_ref[k * 16 : (k + 1) * 16, g * width : (g + 1) * width] for k in range(per_step) for g in range(extra // 16)]
    for owner in range(HALVES):
        for first in range(0, per_step, group):
            members = range(first, first + group)
            doc = jnp.concatenate([metas[k][owner : owner + 1, :cap] + float((k - first) * span) for k in members], axis=1)
            block = jnp.concatenate([metas[k][owner : owner + 1, LANES : LANES + cap] for k in members], axis=1)
            got = picked(doc, first, group)
            for b in range(blocks):
                kept = got * jnp.where(block == float(b), 1.0, 0.0).astype(jnp.bfloat16)
                left[owner, b * nq : (b + 1) * nq, first * cap : (first + group) * cap] = kept
        for b in range(blocks):
            kept = deep_picked * jnp.where(deep_block == float(b + owner * blocks), 1.0, 0.0).astype(jnp.bfloat16)
            left[owner, b * nq : (b + 1) * nq, per_step * cap :] = kept
        right = jnp.concatenate([x_ref[k, owner * cap : (owner + 1) * cap, :] for k in range(per_step)] + deep_rows, axis=0)
        product = jnp.dot(left[owner], right, preferred_element_type=jnp.float32)

        @pl.when(step == 0)
        def _():
            acc[owner] = product

        @pl.when(step > 0)
        def _():
            acc[owner] += product

    @pl.when(step == pl.num_programs(0) - 1)
    def _():
        code_tiles(flip_ref, acc, o_ref, nq=nq, blocks=blocks)


def lean_tiles(flip, queries, rows, *, cap, span, blocks, extra, per_step=8):
    nq = queries.shape[0]
    sources, depth, width = rows.shape
    lanes = blocks * width + LANES
    targets = 16 * HALVES
    deep_lanes = extra // 16 * width
    deep_at = sources * span // deep_lanes
    grid_spec = pltpu.PrefetchScalarGridSpec(
        num_scalar_prefetch=1,
        grid=(sources // per_step,),
        in_specs=[
            pl.BlockSpec((nq, per_step * span), lambda i, _: (0, i)),
            pl.BlockSpec((per_step * 16, deep_lanes), lambda i, _: (i, deep_at)),
            pl.BlockSpec((per_step, depth, width), lambda i, _: (i, 0, 0)),
        ],
        out_specs=pl.BlockSpec((targets, nq // 16, lanes), lambda i, _: (0, 0, 0)),
        scratch_shapes=[
            pltpu.VMEM((HALVES, blocks * nq, per_step * (cap + extra)), jnp.bfloat16),
            pltpu.VMEM((HALVES, blocks * nq, width), jnp.float32),
        ],
    )
    return pl.pallas_call(
        functools.partial(lean_kernel, cap=cap, span=span, per_step=per_step, blocks=blocks, extra=extra),
        grid_spec=grid_spec,
        out_shape=jax.ShapeDtypeStruct((targets, nq // 16, lanes), jnp.int16),
        compiler_params=pltpu.CompilerParams(vmem_limit_bytes=56 << 20),
        cost_estimate=pl.CostEstimate(
            flops=2 * nq * sources * HALVES * (cap + extra) * width * blocks,
            bytes_accessed=2 * (queries.size + rows.size),
            transcendentals=0,
        ),
        name="lean_tiles",
    )(flip, queries, queries, rows)


def gram_kernel(flip_ref, q_ref, x_ref, o_ref, left, acc, *, cap, span, per_step, blocks):
    step = pl.program_id(0)
    width = x_ref.shape[2]
    nq = q_ref.shape[0]
    pair_rows = 2 * cap
    for owner in range(HALVES):
        for pair in range(per_step // 2):
            docs, ids = [], []
            for k in range(2):
                base = HALVES * cap
                meta = x_ref[2 * pair + k, base : base + TILE, :][owner : owner + 1, :].astype(jnp.float32)
                docs.append(meta[:, :cap] + float(k * span))
                ids.append(meta[:, cap : 2 * cap])
            doc = jnp.concatenate(docs, axis=1).astype(jnp.int32)
            block = jnp.concatenate(ids, axis=1)
            rows = lax.broadcasted_iota(jnp.int32, (2 * span, pair_rows), 0)
            chosen = jnp.where(rows == doc, 1.0, 0.0).astype(jnp.bfloat16)
            queries = q_ref[:, pair * 2 * span : (pair + 1) * 2 * span]
            picked = jnp.dot(queries, chosen, preferred_element_type=jnp.float32).astype(jnp.bfloat16)
            for b in range(blocks):
                kept = picked * jnp.where(block == float(b), 1.0, 0.0).astype(jnp.bfloat16)
                left[owner, b * nq : (b + 1) * nq, pair * pair_rows : (pair + 1) * pair_rows] = kept
        right = jnp.concatenate([x_ref[k, owner * cap : (owner + 1) * cap, :] for k in range(per_step)], axis=0)
        product = jnp.dot(left[owner], right, preferred_element_type=jnp.float32)

        @pl.when(step == 0)
        def _():
            acc[owner] = product

        @pl.when(step > 0)
        def _():
            acc[owner] += product

    @pl.when(step == pl.num_programs(0) - 1)
    def _():
        code_tiles(flip_ref, acc, o_ref, nq=nq, blocks=blocks)


def partial_tiles(flip, queries, rows, *, cap, span, blocks, per_step=4):
    nq, docs = queries.shape
    sources, depth, width = rows.shape
    lanes = blocks * width + LANES
    targets = 16 * HALVES
    grid_spec = pltpu.PrefetchScalarGridSpec(
        num_scalar_prefetch=1,
        grid=(sources // per_step,),
        in_specs=[
            pl.BlockSpec((nq, per_step * span), lambda i, _: (0, i)),
            pl.BlockSpec((per_step, depth, width), lambda i, _: (i, 0, 0)),
        ],
        out_specs=pl.BlockSpec((targets, nq // 16, lanes), lambda i, _: (0, 0, 0)),
        scratch_shapes=[
            pltpu.VMEM((HALVES, blocks * nq, per_step * cap), jnp.bfloat16),
            pltpu.VMEM((HALVES, blocks * nq, width), jnp.float32),
        ],
    )
    return pl.pallas_call(
        functools.partial(gram_kernel, cap=cap, span=span, per_step=per_step, blocks=blocks),
        grid_spec=grid_spec,
        out_shape=jax.ShapeDtypeStruct((targets, nq // 16, lanes), jnp.int16),
        compiler_params=pltpu.CompilerParams(vmem_limit_bytes=48 << 20),
        cost_estimate=pl.CostEstimate(
            flops=2 * nq * sources * HALVES * cap * width * blocks,
            bytes_accessed=2 * (queries.size + rows.size),
            transcendentals=0,
        ),
        name="gram_tiles",
    )(flip, queries, rows)


def held_kernel(q_ref, o_ref):
    pltpu.touch(o_ref)


def held(queries):
    return pl.pallas_call(
        held_kernel,
        out_shape=jax.ShapeDtypeStruct(queries.shape, queries.dtype),
        in_specs=[pl.BlockSpec(memory_space=pl.ANY)],
        out_specs=pl.BlockSpec(memory_space=pl.ANY),
        input_output_aliases={0: 0},
        cost_estimate=pl.CostEstimate(flops=10**12, bytes_accessed=10**6, transcendentals=0),
        name="held",
    )(queries)


def sum_kernel(p_ref, o_ref, *, blocks, width):
    groups = p_ref.shape[0]
    scale = jnp.exp2(p_ref[:, :, blocks * width :].astype(jnp.float32) * (1.0 / CODE_STEP))
    for b in range(blocks):
        total = jnp.zeros((p_ref.shape[1], width), jnp.float32)
        for g in range(groups):
            part = p_ref[g, :, b * width : (b + 1) * width].astype(jnp.float32)
            total = total + part * scale[g, :, b : b + 1]
        o_ref[:, b * width : (b + 1) * width] = total


def summed(parts, *, blocks, width):
    return pl.pallas_call(
        functools.partial(sum_kernel, blocks=blocks, width=width),
        out_shape=jax.ShapeDtypeStruct((parts.shape[1], blocks * width), jnp.float32),
        in_specs=[pl.BlockSpec(memory_space=pltpu.VMEM)],
        out_specs=pl.BlockSpec(memory_space=pltpu.VMEM),
        compiler_params=pltpu.CompilerParams(vmem_limit_bytes=16 << 20),
        name="sum_parts",
    )(parts)


def per_device(query_rows, row_values, row_slots, row_counts):
    z_size = lax.axis_size("z")
    owners = HALVES * z_size
    doc_count = query_rows.shape[1]
    span = doc_count // owners
    _, _, _, cap, width = row_values.shape
    blocks = 8
    y = lax.axis_index("y")
    me = y * z_size + lax.axis_index("z")

    half_docs = doc_count // HALVES
    mine = lax.dynamic_slice_in_dim(query_rows, y * half_docs, half_docs, 1)
    theirs = lax.dynamic_slice_in_dim(query_rows, (1 - y) * half_docs, half_docs, 1)
    mirror = lax.ppermute(theirs, "y", [(0, 1), (1, 0)])
    both = jnp.concatenate([mine, mirror], axis=0)

    slots = row_slots[0, 0]
    counts = row_counts[0, 0]
    places = jnp.arange(cap, dtype=jnp.int32)
    live = places[None, :] < counts[:, None]
    doc = slots // blocks - me * span
    block = jnp.where(live, slots % blocks, DEAD)
    flip = y.astype(jnp.int32).reshape(1)

    beyond = jnp.maximum(counts - SHALLOW, 0)
    order = jnp.arange(owners, dtype=jnp.int32)
    before = jnp.sum(jnp.where(order[None, :] < order[:, None], beyond[None, :], 0), axis=1)
    too_many = jnp.sum(beyond) > EXTRA
    depth = cap - SHALLOW
    place = jnp.where(live[:, SHALLOW:], before[:, None] + jnp.arange(depth, dtype=jnp.int32)[None, :], EXTRA)
    place = place.reshape(1, owners * depth)
    taken = place == jnp.arange(EXTRA, dtype=jnp.int32)[:, None]
    deep = row_values[0, 0, :, SHALLOW:, :].reshape(owners * depth, width)
    deep = jnp.dot(taken.astype(jnp.bfloat16), deep, preferred_element_type=jnp.float32).astype(jnp.bfloat16)
    beside = jnp.concatenate([deep[g : g + 16] for g in range(0, EXTRA, 16)], axis=1)
    both = jnp.concatenate([both, beside], axis=1)
    packed = 1 + doc * blocks + slots % blocks + order[:, None] * (span * blocks)
    packed = jnp.sum(jnp.where(taken, packed[:, SHALLOW:].reshape(1, owners * depth), 0), axis=1)

    slots, row_values, both = lax.optimization_barrier((slots, row_values, both))
    values = row_values[0, 0]
    queries = lax.all_gather(both, "z", axis=0, tiled=True)

    fill = jnp.zeros((owners, LANES - SHALLOW), jnp.int32)
    near = jnp.concatenate([doc[:, :SHALLOW], fill, block[:, :SHALLOW], fill], axis=1)
    near = near.reshape(HALVES, z_size, 2 * LANES).transpose(1, 0, 2)
    code = jnp.maximum(packed - 1, 0)
    target = code // (span * blocks)
    ring = jnp.arange(z_size, dtype=jnp.int32)[:, None]
    wanted = (packed > 0)[None, :] & ((target % z_size)[None, :] == ring)
    far_block = jnp.where(wanted, (code % blocks + target // z_size * blocks)[None, :], DEAD)
    far_doc = jnp.broadcast_to((code % (span * blocks)) // blocks, (z_size, EXTRA))
    blank = jnp.zeros((z_size, LANES - EXTRA), jnp.int32)
    far = jnp.concatenate([far_doc, blank, far_block, blank], axis=1)[:, None, :]
    flag = jnp.broadcast_to(too_many.astype(jnp.int32), (z_size, TILE - HALVES - 1, 2 * LANES))
    meta = jnp.concatenate([near, far, flag], axis=1).astype(jnp.bfloat16)
    sent = jnp.concatenate([values[:z_size, :SHALLOW], values[z_size:, :SHALLOW], meta], axis=1)
    rows = lax.all_to_all(sent, "z", split_axis=0, concat_axis=0, tiled=True)

    def lean(queries, rows, row_values):
        return lean_tiles(flip, queries, rows, cap=SHALLOW, span=span, blocks=blocks, extra=EXTRA)

    def full(queries, rows, row_values):
        meta = jnp.concatenate([doc, block], axis=1).reshape(HALVES, z_size, 2 * cap).transpose(1, 0, 2)
        meta = jnp.pad(meta, ((0, 0), (0, TILE - HALVES), (0, 0))).astype(jnp.bfloat16)
        values = row_values[0, 0]
        sent = jnp.concatenate([values[:z_size], values[z_size:], meta], axis=1)
        rows = lax.all_to_all(sent, "z", split_axis=0, concat_axis=0, tiled=True)
        return partial_tiles(flip, queries, rows, cap=cap, span=span, blocks=blocks)

    crowded = jnp.max(rows[:, HALVES * SHALLOW + TILE - 1, 0].astype(jnp.float32)) > 0.5
    coded = lax.cond(crowded, full, lean, held(queries), rows, row_values)
    parts = lax.all_to_all(coded, ("doc", "y"), split_axis=0, concat_axis=0, tiled=True)
    return summed(parts, blocks=blocks, width=width)


def solution(mesh):
    docs, owners = mesh.devices.shape
    split = Mesh(mesh.devices.reshape(docs, HALVES, owners // HALVES), ("doc", "y", "z"))
    blk = ("y", "z")
    in_specs = (
        P(blk, "doc"),
        P("doc", blk, None, None, None),
        P("doc", blk, None, None),
        P("doc", blk, None),
    )
    return jax.shard_map(
        per_device, mesh=split, in_specs=in_specs, out_specs=P("doc", blk), check_vma=False
    )
```

```python
import functools

import jax
import jax.numpy as jnp
from jax import lax
from jax.experimental import pallas as pl
from jax.experimental.pallas import tpu as pltpu
from jax.sharding import Mesh
from jax.sharding import PartitionSpec as P

HALVES = 2
CODE_STEP = 64.0
TOP = 32700.0
TINY = 2.0**-110
LANES = 128
TILE = 8
SHALLOW = 96
EXTRA = 32
DEAD = 64


def code_tiles(flip_ref, acc, o_ref, *, nq, blocks):
    width = acc.shape[2]
    flip = flip_ref[0]
    half = nq // (2 * 16)
    lane = lax.broadcasted_iota(jnp.int32, (16, LANES), 1)

    def tile_of(owner, b, m, slot):
        base = b * nq + m * 32 + slot * 8
        return jnp.concatenate([acc[owner, base : base + 8, :], acc[owner, base + 16 : base + 24, :]], axis=0)

    for owner in range(HALVES):
        for m in range(half):
            for slot in range(2):
                target = ((slot + flip - 2 * slot * flip) * half + m) * HALVES + owner
                peaks = jnp.full((16, LANES), TINY, jnp.float32)
                for b in range(blocks):
                    peak = jnp.max(jnp.abs(tile_of(owner, b, m, slot)), axis=1, keepdims=True)
                    peaks = jnp.where(lane == b, jnp.maximum(peak, TINY), peaks)
                code = jnp.ceil((jnp.log2(peaks) - jnp.log2(TOP)) * CODE_STEP)
                inverse = jnp.exp2(code * (-1.0 / CODE_STEP))
                for b in range(blocks):
                    coded = tile_of(owner, b, m, slot) * inverse[:, b : b + 1]
                    coded = jnp.floor(coded + 0.5).astype(jnp.int32).astype(jnp.int16)
                    o_ref[target, :, b * width : (b + 1) * width] = coded
                o_ref[target, :, blocks * width :] = code.astype(jnp.int32).astype(jnp.int16)


def lean_kernel(flip_ref, q_ref, deep_ref, x_ref, o_ref, left, acc, *, cap, span, per_step, blocks, extra):
    step = pl.program_id(0)
    width = x_ref.shape[2]
    nq = q_ref.shape[0]
    base = HALVES * cap
    window = 2 * LANES
    group = 4
    places = lax.broadcasted_iota(jnp.int32, (window, window), 0)
    picked, blocks_of = [], []
    for k in range(per_step):
        meta = x_ref[k, base : base + TILE, :].astype(jnp.float32)
        start = k * span // LANES * LANES
        doc = meta[0:1, :].astype(jnp.int32) + (k * span - start)
        chosen = jnp.where(places == doc, 1.0, 0.0).astype(jnp.bfloat16)
        queries = q_ref[:, start : start + window]
        picked.append(jnp.dot(queries, chosen, preferred_element_type=jnp.float32).astype(jnp.bfloat16))
        blocks_of.append(meta[1:2, :])
    deep_picked = jnp.concatenate([p[:, base : base + extra] for p in picked], axis=1)
    deep_block = jnp.concatenate([c[:, base : base + extra] for c in blocks_of], axis=1)
    deep_rows = [deep_ref[k * 16 : (k + 1) * 16, g * width : (g + 1) * width] for k in range(per_step) for g in range(extra // 16)]
    for owner in range(HALVES):
        lanes = slice(owner * cap, (owner + 1) * cap)
        for first in range(0, per_step, group):
            got = jnp.concatenate([p[:, lanes] for p in picked[first : first + group]], axis=1)
            block = jnp.concatenate([c[:, lanes] for c in blocks_of[first : first + group]], axis=1)
            for b in range(blocks):
                kept = got * jnp.where(block == float(b), 1.0, 0.0).astype(jnp.bfloat16)
                left[owner, b * nq : (b + 1) * nq, first * cap : (first + group) * cap] = kept
        for b in range(blocks):
            kept = deep_picked * jnp.where(deep_block == float(b + owner * blocks), 1.0, 0.0).astype(jnp.bfloat16)
            left[owner, b * nq : (b + 1) * nq, per_step * cap :] = kept
        right = jnp.concatenate([x_ref[k, lanes, :] for k in range(per_step)] + deep_rows, axis=0)
        product = jnp.dot(left[owner], right, preferred_element_type=jnp.float32)

        @pl.when(step == 0)
        def _():
            acc[owner] = product

        @pl.when(step > 0)
        def _():
            acc[owner] += product

    @pl.when(step == pl.num_programs(0) - 1)
    def _():
        code_tiles(flip_ref, acc, o_ref, nq=nq, blocks=blocks)


def lean_tiles(flip, queries, rows, *, cap, span, blocks, extra, per_step=8):
    nq = queries.shape[0]
    sources, depth, width = rows.shape
    lanes = blocks * width + LANES
    targets = 16 * HALVES
    deep_lanes = extra // 16 * width
    deep_at = sources * span // deep_lanes
    grid_spec = pltpu.PrefetchScalarGridSpec(
        num_scalar_prefetch=1,
        grid=(sources // per_step,),
        in_specs=[
            pl.BlockSpec((nq, per_step * span), lambda i, _: (0, i)),
            pl.BlockSpec((per_step * 16, deep_lanes), lambda i, _: (i, deep_at)),
            pl.BlockSpec((per_step, depth, width), lambda i, _: (i, 0, 0)),
        ],
        out_specs=pl.BlockSpec((targets, nq // 16, lanes), lambda i, _: (0, 0, 0)),
        scratch_shapes=[
            pltpu.VMEM((HALVES, blocks * nq, per_step * (cap + extra)), jnp.bfloat16),
            pltpu.VMEM((HALVES, blocks * nq, width), jnp.float32),
        ],
    )
    return pl.pallas_call(
        functools.partial(lean_kernel, cap=cap, span=span, per_step=per_step, blocks=blocks, extra=extra),
        grid_spec=grid_spec,
        out_shape=jax.ShapeDtypeStruct((targets, nq // 16, lanes), jnp.int16),
        compiler_params=pltpu.CompilerParams(vmem_limit_bytes=56 << 20),
        cost_estimate=pl.CostEstimate(
            flops=2 * nq * sources * HALVES * (cap + extra) * width * blocks,
            bytes_accessed=2 * (queries.size + rows.size),
            transcendentals=0,
        ),
        name="lean_tiles",
    )(flip, queries, queries, rows)


def gram_kernel(flip_ref, q_ref, x_ref, o_ref, left, acc, *, cap, span, per_step, blocks):
    step = pl.program_id(0)
    width = x_ref.shape[2]
    nq = q_ref.shape[0]
    pair_rows = 2 * cap
    for owner in range(HALVES):
        for pair in range(per_step // 2):
            docs, ids = [], []
            for k in range(2):
                base = HALVES * cap
                meta = x_ref[2 * pair + k, base : base + TILE, :][owner : owner + 1, :].astype(jnp.float32)
                docs.append(meta[:, :cap] + float(k * span))
                ids.append(meta[:, cap : 2 * cap])
            doc = jnp.concatenate(docs, axis=1).astype(jnp.int32)
            block = jnp.concatenate(ids, axis=1)
            rows = lax.broadcasted_iota(jnp.int32, (2 * span, pair_rows), 0)
            chosen = jnp.where(rows == doc, 1.0, 0.0).astype(jnp.bfloat16)
            queries = q_ref[:, pair * 2 * span : (pair + 1) * 2 * span]
            picked = jnp.dot(queries, chosen, preferred_element_type=jnp.float32).astype(jnp.bfloat16)
            for b in range(blocks):
                kept = picked * jnp.where(block == float(b), 1.0, 0.0).astype(jnp.bfloat16)
                left[owner, b * nq : (b + 1) * nq, pair * pair_rows : (pair + 1) * pair_rows] = kept
        right = jnp.concatenate([x_ref[k, owner * cap : (owner + 1) * cap, :] for k in range(per_step)], axis=0)
        product = jnp.dot(left[owner], right, preferred_element_type=jnp.float32)

        @pl.when(step == 0)
        def _():
            acc[owner] = product

        @pl.when(step > 0)
        def _():
            acc[owner] += product

    @pl.when(step == pl.num_programs(0) - 1)
    def _():
        code_tiles(flip_ref, acc, o_ref, nq=nq, blocks=blocks)


def partial_tiles(flip, queries, rows, *, cap, span, blocks, per_step=4):
    nq, docs = queries.shape
    sources, depth, width = rows.shape
    lanes = blocks * width + LANES
    targets = 16 * HALVES
    grid_spec = pltpu.PrefetchScalarGridSpec(
        num_scalar_prefetch=1,
        grid=(sources // per_step,),
        in_specs=[
            pl.BlockSpec((nq, per_step * span), lambda i, _: (0, i)),
            pl.BlockSpec((per_step, depth, width), lambda i, _: (i, 0, 0)),
        ],
        out_specs=pl.BlockSpec((targets, nq // 16, lanes), lambda i, _: (0, 0, 0)),
        scratch_shapes=[
            pltpu.VMEM((HALVES, blocks * nq, per_step * cap), jnp.bfloat16),
            pltpu.VMEM((HALVES, blocks * nq, width), jnp.float32),
        ],
    )
    return pl.pallas_call(
        functools.partial(gram_kernel, cap=cap, span=span, per_step=per_step, blocks=blocks),
        grid_spec=grid_spec,
        out_shape=jax.ShapeDtypeStruct((targets, nq // 16, lanes), jnp.int16),
        compiler_params=pltpu.CompilerParams(vmem_limit_bytes=48 << 20),
        cost_estimate=pl.CostEstimate(
            flops=2 * nq * sources * HALVES * cap * width * blocks,
            bytes_accessed=2 * (queries.size + rows.size),
            transcendentals=0,
        ),
        name="gram_tiles",
    )(flip, queries, rows)


def payload_kernel(counts_ref, info_ref, slots_ref, far_ref, low_ref, high_ref, o_ref, *, shallow, extra, blocks):
    step = pl.program_id(0)
    here, z_size = low_ref.shape[0], low_ref.shape[0] * pl.num_programs(0)
    lane = lax.broadcasted_iota(jnp.int32, (1, slots_ref.shape[1]), 1)
    base = HALVES * shallow
    rest = o_ref.shape[2] - base - extra
    for r in range(here):
        z = step * here + r
        docs, ids = [], []
        for half in range(HALVES):
            owner = half * z_size + z
            slots = slots_ref[pl.ds(owner, 1), :]
            doc = lax.shift_right_logical(slots, blocks.bit_length() - 1) - info_ref[0]
            block = jnp.where(lane < counts_ref[owner], slots & (blocks - 1), DEAD)
            docs.append(doc[:, :shallow].astype(jnp.float32))
            ids.append(block[:, :shallow].astype(jnp.float32))
        far = jnp.where(far_ref[2:3, :] == z, far_ref[1:2, :], DEAD)
        docs.append(far_ref[0:1, :extra].astype(jnp.float32))
        ids.append(far[:, :extra].astype(jnp.float32))
        docs.append(jnp.zeros((1, rest), jnp.float32))
        ids.append(jnp.full((1, rest), float(DEAD), jnp.float32))
        flag = jnp.full((TILE - 2, o_ref.shape[2]), info_ref[1].astype(jnp.float32))
        meta = jnp.concatenate([jnp.concatenate(docs, axis=1), jnp.concatenate(ids, axis=1), flag], axis=0)
        o_ref[r, :shallow, :] = low_ref[r, :shallow, :]
        o_ref[r, shallow:base, :] = high_ref[r, :shallow, :]
        o_ref[r, base:, :] = meta.astype(jnp.bfloat16)


def payload(counts, info, slots, far, values, *, blocks, per_step=4):
    owners, cap, width = values.shape
    z_size = owners // HALVES
    depth = HALVES * SHALLOW + TILE
    steps = z_size // per_step
    grid_spec = pltpu.PrefetchScalarGridSpec(
        num_scalar_prefetch=2,
        grid=(steps,),
        in_specs=[
            pl.BlockSpec(slots.shape, lambda i, *_: (0, 0)),
            pl.BlockSpec(far.shape, lambda i, *_: (0, 0)),
            pl.BlockSpec((per_step, cap, width), lambda i, *_: (i, 0, 0)),
            pl.BlockSpec((per_step, cap, width), lambda i, *_: (i + steps, 0, 0)),
        ],
        out_specs=pl.BlockSpec((per_step, depth, width), lambda i, *_: (i, 0, 0)),
    )
    return pl.pallas_call(
        functools.partial(payload_kernel, shallow=SHALLOW, extra=EXTRA, blocks=blocks),
        grid_spec=grid_spec,
        out_shape=jax.ShapeDtypeStruct((z_size, depth, width), jnp.bfloat16),
        compiler_params=pltpu.CompilerParams(vmem_limit_bytes=16 << 20),
        cost_estimate=pl.CostEstimate(flops=0, bytes_accessed=4 * values.size, transcendentals=0),
        name="payload",
    )(counts, info, slots, far, values, values)


def held_kernel(q_ref, o_ref):
    pltpu.touch(o_ref)


def held(queries):
    return pl.pallas_call(
        held_kernel,
        out_shape=jax.ShapeDtypeStruct(queries.shape, queries.dtype),
        in_specs=[pl.BlockSpec(memory_space=pl.ANY)],
        out_specs=pl.BlockSpec(memory_space=pl.ANY),
        input_output_aliases={0: 0},
        cost_estimate=pl.CostEstimate(flops=10**12, bytes_accessed=10**6, transcendentals=0),
        name="held",
    )(queries)


def sum_kernel(p_ref, o_ref, *, blocks, width):
    groups = p_ref.shape[0]
    scale = jnp.exp2(p_ref[:, :, blocks * width :].astype(jnp.float32) * (1.0 / CODE_STEP))
    for b in range(blocks):
        total = jnp.zeros((p_ref.shape[1], width), jnp.float32)
        for g in range(groups):
            part = p_ref[g, :, b * width : (b + 1) * width].astype(jnp.float32)
            total = total + part * scale[g, :, b : b + 1]
        o_ref[:, b * width : (b + 1) * width] = total


def summed(parts, *, blocks, width):
    return pl.pallas_call(
        functools.partial(sum_kernel, blocks=blocks, width=width),
        out_shape=jax.ShapeDtypeStruct((parts.shape[1], blocks * width), jnp.float32),
        in_specs=[pl.BlockSpec(memory_space=pltpu.VMEM)],
        out_specs=pl.BlockSpec(memory_space=pltpu.VMEM),
        compiler_params=pltpu.CompilerParams(vmem_limit_bytes=16 << 20),
        name="sum_parts",
    )(parts)


def per_device(query_rows, row_values, row_slots, row_counts):
    z_size = lax.axis_size("z")
    owners = HALVES * z_size
    doc_count = query_rows.shape[1]
    span = doc_count // owners
    _, _, _, cap, width = row_values.shape
    blocks = 8
    y = lax.axis_index("y")
    me = y * z_size + lax.axis_index("z")

    half_docs = doc_count // HALVES
    mine = lax.dynamic_slice_in_dim(query_rows, y * half_docs, half_docs, 1)
    theirs = lax.dynamic_slice_in_dim(query_rows, (1 - y) * half_docs, half_docs, 1)
    mirror = lax.ppermute(theirs, "y", [(0, 1), (1, 0)])
    both = jnp.concatenate([mine, mirror], axis=0)

    slots = row_slots[0, 0]
    counts = row_counts[0, 0]
    places = jnp.arange(cap, dtype=jnp.int32)
    live = places[None, :] < counts[:, None]
    doc = slots // blocks - me * span
    block = jnp.where(live, slots % blocks, DEAD)
    flip = y.astype(jnp.int32).reshape(1)

    beyond = jnp.maximum(counts - SHALLOW, 0)
    order = jnp.arange(owners, dtype=jnp.int32)
    before = jnp.sum(jnp.where(order[None, :] < order[:, None], beyond[None, :], 0), axis=1)
    too_many = jnp.sum(beyond) > EXTRA
    depth = cap - SHALLOW
    place = jnp.where(live[:, SHALLOW:], before[:, None] + jnp.arange(depth, dtype=jnp.int32)[None, :], EXTRA)
    place = place.reshape(1, owners * depth)
    taken = place == jnp.arange(EXTRA, dtype=jnp.int32)[:, None]
    deep = row_values[0, 0, :, SHALLOW:, :].reshape(owners * depth, width)
    deep = jnp.dot(taken.astype(jnp.bfloat16), deep, preferred_element_type=jnp.float32).astype(jnp.bfloat16)
    beside = jnp.concatenate([deep[g : g + 16] for g in range(0, EXTRA, 16)], axis=1)
    both = jnp.concatenate([both, beside], axis=1)
    packed = 1 + doc * blocks + slots % blocks + order[:, None] * (span * blocks)
    packed = jnp.sum(jnp.where(taken, packed[:, SHALLOW:].reshape(1, owners * depth), 0), axis=1)

    slots, row_values, both = lax.optimization_barrier((slots, row_values, both))
    queries = lax.all_gather(both, "z", axis=0, tiled=True)

    code = jnp.maximum(packed - 1, 0)
    target = code // (span * blocks)
    far = jnp.stack([
        code % (span * blocks) // blocks,
        code % blocks + target // z_size * blocks,
        jnp.where(packed > 0, target % z_size, z_size),
    ])
    far = jnp.pad(far, ((0, TILE - 3), (0, LANES - EXTRA)))
    info = jnp.stack([me * span, too_many.astype(jnp.int32)])
    sent = payload(counts, info, slots, far, row_values[0, 0], blocks=blocks)
    rows = lax.all_to_all(sent, "z", split_axis=0, concat_axis=0, tiled=True)

    def lean(queries, rows, row_values):
        return lean_tiles(flip, queries, rows, cap=SHALLOW, span=span, blocks=blocks, extra=EXTRA)

    def full(queries, rows, row_values):
        meta = jnp.concatenate([doc, block], axis=1).reshape(HALVES, z_size, 2 * cap).transpose(1, 0, 2)
        meta = jnp.pad(meta, ((0, 0), (0, TILE - HALVES), (0, 0))).astype(jnp.bfloat16)
        values = row_values[0, 0]
        sent = jnp.concatenate([values[:z_size], values[z_size:], meta], axis=1)
        rows = lax.all_to_all(sent, "z", split_axis=0, concat_axis=0, tiled=True)
        return partial_tiles(flip, queries, rows, cap=cap, span=span, blocks=blocks)

    crowded = jnp.max(rows[:, HALVES * SHALLOW + TILE - 1, 0].astype(jnp.float32)) > 0.5
    coded = lax.cond(crowded, full, lean, held(queries), rows, row_values)
    parts = lax.all_to_all(coded, ("doc", "y"), split_axis=0, concat_axis=0, tiled=True)
    return summed(parts, blocks=blocks, width=width)


def solution(mesh):
    docs, owners = mesh.devices.shape
    split = Mesh(mesh.devices.reshape(docs, HALVES, owners // HALVES), ("doc", "y", "z"))
    blk = ("y", "z")
    in_specs = (
        P(blk, "doc"),
        P("doc", blk, None, None, None),
        P("doc", blk, None, None),
        P("doc", blk, None),
    )
    return jax.shard_map(
        per_device, mesh=split, in_specs=in_specs, out_specs=P("doc", blk), check_vma=False
    )
```

```python
import functools

import jax
import jax.numpy as jnp
from jax import lax
from jax.experimental import pallas as pl
from jax.experimental.pallas import tpu as pltpu
from jax.sharding import Mesh
from jax.sharding import PartitionSpec as P

HALVES = 2
CODE_STEP = 64.0
TOP = 32700.0
TINY = 2.0**-110
LANES = 128
TILE = 8
SHALLOW = 96
EXTRA = 32
DEAD = 64


def code_tiles(flip_ref, acc, o_ref, *, nq, blocks):
    width = acc.shape[2]
    flip = flip_ref[0]
    half = nq // (2 * 16)
    lane = lax.broadcasted_iota(jnp.int32, (16, LANES), 1)

    def tile_of(owner, b, m, slot):
        base = b * nq + m * 32 + slot * 8
        return jnp.concatenate([acc[owner, base : base + 8, :], acc[owner, base + 16 : base + 24, :]], axis=0)

    for owner in range(HALVES):
        for m in range(half):
            for slot in range(2):
                target = ((slot + flip - 2 * slot * flip) * half + m) * HALVES + owner
                peaks = jnp.full((16, LANES), TINY, jnp.float32)
                for b in range(blocks):
                    peak = jnp.max(jnp.abs(tile_of(owner, b, m, slot)), axis=1, keepdims=True)
                    peaks = jnp.where(lane == b, jnp.maximum(peak, TINY), peaks)
                code = jnp.ceil((jnp.log2(peaks) - jnp.log2(TOP)) * CODE_STEP)
                inverse = jnp.exp2(code * (-1.0 / CODE_STEP))
                for b in range(blocks):
                    coded = tile_of(owner, b, m, slot) * inverse[:, b : b + 1]
                    coded = jnp.floor(coded + 0.5).astype(jnp.int32).astype(jnp.int16)
                    o_ref[target, :, b * width : (b + 1) * width] = coded
                o_ref[target, :, blocks * width :] = code.astype(jnp.int32).astype(jnp.int16)


def lean_kernel(place_ref, q_ref, deep_ref, far_ref, x_ref, o_ref, left, acc, right_ref, *, cap, span, per_step, blocks, extra):
    step = pl.program_id(0)
    width = x_ref.shape[2]
    nq = q_ref.shape[0]
    base = HALVES * cap
    window = 2 * LANES
    tall = blocks * nq
    lane = lax.broadcasted_iota(jnp.int32, (1, LANES), 1)

    @pl.when(step == 0)
    def _():
        acc[...] = jnp.zeros_like(acc)

    places = lax.broadcasted_iota(jnp.int32, (window, window), 0)
    for k in range(per_step):
        meta = x_ref[k, base : base + TILE, :].astype(jnp.float32)
        far = far_ref[k * 16 : k * 16 + TILE, :].astype(jnp.float32)
        docs, ids = [], []
        for owner in range(HALVES):
            lanes = slice(owner * LANES, (owner + 1) * LANES)
            to_owner = far[2:3, :] == (place_ref[1] + owner * place_ref[2]).astype(jnp.float32)
            docs.append(jnp.where(lane < cap, meta[0:1, lanes], far[0:1, :]))
            ids.append(jnp.where(lane < cap, meta[1:2, lanes], jnp.where(to_owner, far[1:2, :], float(DEAD))))
        start = k * span // LANES * LANES
        doc = jnp.concatenate(docs, axis=1).astype(jnp.int32) + (k * span - start)
        chosen = jnp.where(places == doc, 1.0, 0.0).astype(jnp.bfloat16)
        queries = q_ref[:, start : start + window]
        picked = jnp.dot(queries, chosen, preferred_element_type=jnp.float32).astype(jnp.bfloat16)
        for owner in range(HALVES):
            lanes = slice(owner * LANES, (owner + 1) * LANES)
            for b in range(blocks):
                kept = picked[:, lanes] * jnp.where(ids[owner] == float(b), 1.0, 0.0).astype(jnp.bfloat16)
                left[owner * tall + b * nq : owner * tall + (b + 1) * nq, k * LANES : (k + 1) * LANES] = kept
    for owner in range(HALVES):
        right = []
        for k in range(per_step):
            right.append(x_ref[k, owner * cap : (owner + 1) * cap, :])
            right += [deep_ref[k * 16 : (k + 1) * 16, g * width : (g + 1) * width] for g in range(extra // 16)]
        right = jnp.concatenate(right, axis=0)
        right_ref[...] = right
        acc[owner] += jnp.dot(left[owner * tall : (owner + 1) * tall, :], right_ref[...], preferred_element_type=jnp.float32)

    @pl.when(step == pl.num_programs(0) - 1)
    def _():
        code_tiles(place_ref, acc, o_ref, nq=nq, blocks=blocks)


def lean_tiles(place, queries, rows, *, cap, span, blocks, extra, per_step=8):
    nq = queries.shape[0]
    sources, depth, width = rows.shape
    lanes = blocks * width + LANES
    targets = 16 * HALVES
    deep_lanes = extra // 16 * width
    deep_at = sources * span // deep_lanes
    far_at = (deep_at + 1) * deep_lanes // LANES
    grid_spec = pltpu.PrefetchScalarGridSpec(
        num_scalar_prefetch=1,
        grid=(sources // per_step,),
        in_specs=[
            pl.BlockSpec((nq, per_step * span), lambda i, _: (0, i)),
            pl.BlockSpec((per_step * 16, deep_lanes), lambda i, _: (i, deep_at)),
            pl.BlockSpec((per_step * 16, LANES), lambda i, _: (i, far_at)),
            pl.BlockSpec((per_step, depth, width), lambda i, _: (i, 0, 0)),
        ],
        out_specs=pl.BlockSpec((targets, nq // 16, lanes), lambda i, _: (0, 0, 0)),
        scratch_shapes=[
            pltpu.VMEM((HALVES * blocks * nq, per_step * (cap + extra)), jnp.bfloat16),
            pltpu.VMEM((HALVES, blocks * nq, width), jnp.float32),
            pltpu.VMEM((per_step * (cap + extra), width), jnp.bfloat16),
        ],
    )
    return pl.pallas_call(
        functools.partial(lean_kernel, cap=cap, span=span, per_step=per_step, blocks=blocks, extra=extra),
        grid_spec=grid_spec,
        out_shape=jax.ShapeDtypeStruct((targets, nq // 16, lanes), jnp.int16),
        compiler_params=pltpu.CompilerParams(vmem_limit_bytes=56 << 20),
        cost_estimate=pl.CostEstimate(
            flops=2 * nq * sources * HALVES * (cap + extra) * width * blocks,
            bytes_accessed=2 * (queries.size + rows.size),
            transcendentals=0,
        ),
        name="lean_tiles",
    )(place, queries, queries, queries, rows)


def gram_kernel(flip_ref, q_ref, x_ref, o_ref, left, acc, *, cap, span, per_step, blocks):
    step = pl.program_id(0)
    width = x_ref.shape[2]
    nq = q_ref.shape[0]
    pair_rows = 2 * cap
    for owner in range(HALVES):
        for pair in range(per_step // 2):
            docs, ids = [], []
            for k in range(2):
                base = HALVES * cap
                meta = x_ref[2 * pair + k, base : base + TILE, :][owner : owner + 1, :].astype(jnp.float32)
                docs.append(meta[:, :cap] + float(k * span))
                ids.append(meta[:, cap : 2 * cap])
            doc = jnp.concatenate(docs, axis=1).astype(jnp.int32)
            block = jnp.concatenate(ids, axis=1)
            rows = lax.broadcasted_iota(jnp.int32, (2 * span, pair_rows), 0)
            chosen = jnp.where(rows == doc, 1.0, 0.0).astype(jnp.bfloat16)
            queries = q_ref[:, pair * 2 * span : (pair + 1) * 2 * span]
            picked = jnp.dot(queries, chosen, preferred_element_type=jnp.float32).astype(jnp.bfloat16)
            for b in range(blocks):
                kept = picked * jnp.where(block == float(b), 1.0, 0.0).astype(jnp.bfloat16)
                left[owner, b * nq : (b + 1) * nq, pair * pair_rows : (pair + 1) * pair_rows] = kept
        right = jnp.concatenate([x_ref[k, owner * cap : (owner + 1) * cap, :] for k in range(per_step)], axis=0)
        product = jnp.dot(left[owner], right, preferred_element_type=jnp.float32)

        @pl.when(step == 0)
        def _():
            acc[owner] = product

        @pl.when(step > 0)
        def _():
            acc[owner] += product

    @pl.when(step == pl.num_programs(0) - 1)
    def _():
        code_tiles(flip_ref, acc, o_ref, nq=nq, blocks=blocks)


def partial_tiles(flip, queries, rows, *, cap, span, blocks, per_step=4):
    nq, docs = queries.shape
    sources, depth, width = rows.shape
    lanes = blocks * width + LANES
    targets = 16 * HALVES
    grid_spec = pltpu.PrefetchScalarGridSpec(
        num_scalar_prefetch=1,
        grid=(sources // per_step,),
        in_specs=[
            pl.BlockSpec((nq, per_step * span), lambda i, _: (0, i)),
            pl.BlockSpec((per_step, depth, width), lambda i, _: (i, 0, 0)),
        ],
        out_specs=pl.BlockSpec((targets, nq // 16, lanes), lambda i, _: (0, 0, 0)),
        scratch_shapes=[
            pltpu.VMEM((HALVES, blocks * nq, per_step * cap), jnp.bfloat16),
            pltpu.VMEM((HALVES, blocks * nq, width), jnp.float32),
        ],
    )
    return pl.pallas_call(
        functools.partial(gram_kernel, cap=cap, span=span, per_step=per_step, blocks=blocks),
        grid_spec=grid_spec,
        out_shape=jax.ShapeDtypeStruct((targets, nq // 16, lanes), jnp.int16),
        compiler_params=pltpu.CompilerParams(vmem_limit_bytes=48 << 20),
        cost_estimate=pl.CostEstimate(
            flops=2 * nq * sources * HALVES * cap * width * blocks,
            bytes_accessed=2 * (queries.size + rows.size),
            transcendentals=0,
        ),
        name="gram_tiles",
    )(flip, queries, rows)


def payload_kernel(counts_ref, first_ref, slots_ref, low_ref, high_ref, o_ref, *, shallow, blocks):
    step = pl.program_id(0)
    here, z_size = low_ref.shape[0], low_ref.shape[0] * pl.num_programs(0)
    lane = lax.broadcasted_iota(jnp.int32, (1, slots_ref.shape[1]), 1)
    base = HALVES * shallow
    for r in range(here):
        z = step * here + r
        docs, ids = [], []
        for half in range(HALVES):
            owner = half * z_size + z
            slots = slots_ref[pl.ds(owner, 1), :]
            doc = lax.shift_right_logical(slots, blocks.bit_length() - 1) - first_ref[0]
            docs.append(doc.astype(jnp.float32))
            ids.append(jnp.where(lane < counts_ref[owner], slots & (blocks - 1), DEAD).astype(jnp.float32))
        rest = jnp.zeros((TILE - 2, o_ref.shape[2]), jnp.float32)
        meta = jnp.concatenate([jnp.concatenate(docs, axis=1), jnp.concatenate(ids, axis=1), rest], axis=0)
        o_ref[r, :shallow, :] = low_ref[r, :shallow, :]
        o_ref[r, shallow:base, :] = high_ref[r, :shallow, :]
        o_ref[r, base:, :] = meta.astype(jnp.bfloat16)


def payload(counts, first, slots, values, *, blocks, per_step=4):
    owners, cap, width = values.shape
    z_size = owners // HALVES
    depth = HALVES * SHALLOW + TILE
    steps = z_size // per_step
    grid_spec = pltpu.PrefetchScalarGridSpec(
        num_scalar_prefetch=2,
        grid=(steps,),
        in_specs=[
            pl.BlockSpec(slots.shape, lambda i, *_: (0, 0)),
            pl.BlockSpec((per_step, cap, width), lambda i, *_: (i, 0, 0)),
            pl.BlockSpec((per_step, cap, width), lambda i, *_: (i + steps, 0, 0)),
        ],
        out_specs=pl.BlockSpec((per_step, depth, width), lambda i, *_: (i, 0, 0)),
    )
    return pl.pallas_call(
        functools.partial(payload_kernel, shallow=SHALLOW, blocks=blocks),
        grid_spec=grid_spec,
        out_shape=jax.ShapeDtypeStruct((z_size, depth, width), jnp.bfloat16),
        compiler_params=pltpu.CompilerParams(vmem_limit_bytes=16 << 20),
        cost_estimate=pl.CostEstimate(flops=0, bytes_accessed=4 * values.size, transcendentals=0),
        name="payload",
    )(counts, first, slots, values, values)


def sum_kernel(p_ref, o_ref, *, blocks, width):
    groups = p_ref.shape[0]
    scale = jnp.exp2(p_ref[:, :, blocks * width :].astype(jnp.float32) * (1.0 / CODE_STEP))
    for b in range(blocks):
        total = jnp.zeros((p_ref.shape[1], width), jnp.float32)
        for g in range(groups):
            part = p_ref[g, :, b * width : (b + 1) * width].astype(jnp.float32)
            total = total + part * scale[g, :, b : b + 1]
        o_ref[:, b * width : (b + 1) * width] = total


def summed(parts, *, blocks, width):
    return pl.pallas_call(
        functools.partial(sum_kernel, blocks=blocks, width=width),
        out_shape=jax.ShapeDtypeStruct((parts.shape[1], blocks * width), jnp.float32),
        in_specs=[pl.BlockSpec(memory_space=pltpu.VMEM)],
        out_specs=pl.BlockSpec(memory_space=pltpu.VMEM),
        compiler_params=pltpu.CompilerParams(vmem_limit_bytes=16 << 20),
        name="sum_parts",
    )(parts)


def per_device(query_rows, row_values, row_slots, row_counts):
    z_size = lax.axis_size("z")
    owners = HALVES * z_size
    doc_count = query_rows.shape[1]
    span = doc_count // owners
    _, _, _, cap, width = row_values.shape
    blocks = 8
    y = lax.axis_index("y")
    me = y * z_size + lax.axis_index("z")

    slots = row_slots[0, 0]
    counts = row_counts[0, 0]
    sent = payload(counts, (me * span).reshape(1), slots, row_values[0, 0], blocks=blocks)
    rows = lax.all_to_all(sent, "z", split_axis=0, concat_axis=0, tiled=True)

    half_docs = doc_count // HALVES
    mine = lax.dynamic_slice_in_dim(query_rows, y * half_docs, half_docs, 1)
    theirs = lax.dynamic_slice_in_dim(query_rows, (1 - y) * half_docs, half_docs, 1)
    mirror = lax.ppermute(theirs, "y", [(0, 1), (1, 0)])

    live = jnp.arange(cap, dtype=jnp.int32)[None, :] < counts[:, None]
    doc = slots // blocks - me * span
    beyond = jnp.maximum(counts - SHALLOW, 0)
    order = jnp.arange(owners, dtype=jnp.int32)
    before = jnp.sum(jnp.where(order[None, :] < order[:, None], beyond[None, :], 0), axis=1)
    too_many = jnp.sum(beyond) > EXTRA
    depth = cap - SHALLOW
    place = jnp.where(live[:, SHALLOW:], before[:, None] + jnp.arange(depth, dtype=jnp.int32)[None, :], EXTRA)
    place = place.reshape(1, owners * depth)
    taken = place == jnp.arange(EXTRA, dtype=jnp.int32)[:, None]
    deep = row_values[0, 0, :, SHALLOW:, :].reshape(owners * depth, width)
    deep = jnp.dot(taken.astype(jnp.bfloat16), deep, preferred_element_type=jnp.float32).astype(jnp.bfloat16)
    packed = 1 + doc * blocks + slots % blocks + order[:, None] * (span * blocks)
    packed = jnp.sum(jnp.where(taken, packed[:, SHALLOW:].reshape(1, owners * depth), 0), axis=1)
    code = jnp.maximum(packed - 1, 0)
    target = jnp.where(packed > 0, code // (span * blocks), DEAD)
    flag = jnp.broadcast_to(too_many.astype(jnp.int32), (EXTRA,))
    far = jnp.stack([code % (span * blocks) // blocks, code % blocks, target, flag]).astype(jnp.bfloat16)
    far = jnp.pad(far, ((0, 16 - 4), (SHALLOW, LANES - SHALLOW - EXTRA)))
    beside = jnp.concatenate([deep[g : g + 16] for g in range(0, EXTRA, 16)] + [far], axis=1)
    both = jnp.concatenate([jnp.concatenate([mine, mirror], axis=0), beside], axis=1)
    queries = lax.all_gather(both, "z", axis=0, tiled=True)
    flip = y.astype(jnp.int32).reshape(1)

    def lean(queries, rows, row_values):
        place = jnp.stack([y, lax.axis_index("z"), z_size]).astype(jnp.int32)
        return lean_tiles(place, queries, rows, cap=SHALLOW, span=span, blocks=blocks, extra=EXTRA)

    def full(queries, rows, row_values):
        block = jnp.where(live, slots % blocks, DEAD)
        meta = jnp.concatenate([doc, block], axis=1).reshape(HALVES, z_size, 2 * cap).transpose(1, 0, 2)
        meta = jnp.pad(meta, ((0, 0), (0, TILE - HALVES), (0, 0))).astype(jnp.bfloat16)
        values = row_values[0, 0]
        sent = jnp.concatenate([values[:z_size], values[z_size:], meta], axis=1)
        rows = lax.all_to_all(sent, "z", split_axis=0, concat_axis=0, tiled=True)
        return partial_tiles(flip, queries, rows, cap=cap, span=span, blocks=blocks)

    flags = queries[:, -LANES:].reshape(z_size, 16, LANES)[:, 3, SHALLOW]
    crowded = jnp.max(flags.astype(jnp.float32)) > 0.5
    coded = lax.cond(crowded, full, lean, queries, rows, row_values)
    parts = lax.all_to_all(coded, ("doc", "y"), split_axis=0, concat_axis=0, tiled=True)
    return summed(parts, blocks=blocks, width=width)


def solution(mesh):
    docs, owners = mesh.devices.shape
    split = Mesh(mesh.devices.reshape(docs, HALVES, owners // HALVES), ("doc", "y", "z"))
    blk = ("y", "z")
    in_specs = (
        P(blk, "doc"),
        P("doc", blk, None, None, None),
        P("doc", blk, None, None),
        P("doc", blk, None),
    )
    return jax.shard_map(
        per_device, mesh=split, in_specs=in_specs, out_specs=P("doc", blk), check_vma=False
    )
```

```python
import functools

import jax
import jax.numpy as jnp
from jax import lax
from jax.experimental import pallas as pl
from jax.experimental.pallas import tpu as pltpu
from jax.sharding import Mesh
from jax.sharding import PartitionSpec as P

HALVES = 2
CODE_STEP = 64.0
TOP = 32700.0
TINY = 2.0**-110
LANES = 128
TILE = 8
SHALLOW = 96
EXTRA = 32
DEAD = 64


def code_tiles(flip_ref, acc, o_ref, *, nq, blocks):
    width = acc.shape[2]
    flip = flip_ref[0]
    half = nq // (2 * 16)
    lane = lax.broadcasted_iota(jnp.int32, (16, LANES), 1)

    def tile_of(owner, b, m, slot):
        base = b * nq + m * 32 + slot * 8
        return jnp.concatenate([acc[owner, base : base + 8, :], acc[owner, base + 16 : base + 24, :]], axis=0)

    for owner in range(HALVES):
        for m in range(half):
            for slot in range(2):
                target = ((slot + flip - 2 * slot * flip) * half + m) * HALVES + owner
                peaks = jnp.full((16, LANES), TINY, jnp.float32)
                for b in range(blocks):
                    peak = jnp.max(jnp.abs(tile_of(owner, b, m, slot)), axis=1, keepdims=True)
                    peaks = jnp.where(lane == b, jnp.maximum(peak, TINY), peaks)
                code = jnp.ceil((jnp.log2(peaks) - jnp.log2(TOP)) * CODE_STEP)
                inverse = jnp.exp2(code * (-1.0 / CODE_STEP))
                for b in range(blocks):
                    coded = tile_of(owner, b, m, slot) * inverse[:, b : b + 1]
                    coded = jnp.floor(coded + 0.5).astype(jnp.int32).astype(jnp.int16)
                    o_ref[target, :, b * width : (b + 1) * width] = coded
                o_ref[target, :, blocks * width :] = code.astype(jnp.int32).astype(jnp.int16)


def lean_kernel(place_ref, q_ref, deep_ref, far_ref, x_ref, o_ref, left, acc, right_ref, *, cap, span, per_step, blocks, extra):
    step = pl.program_id(0)
    width = x_ref.shape[2]
    nq = q_ref.shape[0]
    base = HALVES * cap
    window = 2 * LANES
    tall = blocks * nq
    lane = lax.broadcasted_iota(jnp.int32, (1, LANES), 1)

    @pl.when(step == 0)
    def _():
        acc[...] = jnp.zeros_like(acc)

    places = lax.broadcasted_iota(jnp.int32, (window, window), 0)
    for k in range(per_step):
        meta = x_ref[k, base : base + TILE, :].astype(jnp.float32)
        behind = (per_step - 1 - k) * 16
        far = far_ref[behind : behind + TILE, :].astype(jnp.float32)
        docs, ids = [], []
        for owner in range(HALVES):
            lanes = slice(owner * LANES, (owner + 1) * LANES)
            to_owner = far[2:3, :] == (place_ref[1] + owner * place_ref[2]).astype(jnp.float32)
            docs.append(jnp.where(lane < cap, meta[0:1, lanes], far[0:1, :]))
            ids.append(jnp.where(lane < cap, meta[1:2, lanes], jnp.where(to_owner, far[1:2, :], float(DEAD))))
        start = k * span // LANES * LANES
        doc = jnp.concatenate(docs, axis=1).astype(jnp.int32) + (k * span - start)
        chosen = jnp.where(places == doc, 1.0, 0.0).astype(jnp.bfloat16)
        queries = q_ref[:, start : start + window]
        picked = jnp.dot(queries, chosen, preferred_element_type=jnp.float32).astype(jnp.bfloat16)
        for owner in range(HALVES):
            lanes = slice(owner * LANES, (owner + 1) * LANES)
            for b in range(blocks):
                kept = picked[:, lanes] * jnp.where(ids[owner] == float(b), 1.0, 0.0).astype(jnp.bfloat16)
                left[owner * tall + b * nq : owner * tall + (b + 1) * nq, k * LANES : (k + 1) * LANES] = kept
    for owner in range(HALVES):
        right = []
        for k in range(per_step):
            right.append(x_ref[k, owner * cap : (owner + 1) * cap, :])
            behind = (per_step - 1 - k) * 16
            right += [deep_ref[behind : behind + 16, g * width : (g + 1) * width] for g in range(extra // 16)]
        right = jnp.concatenate(right, axis=0)
        right_ref[...] = right
        acc[owner] += jnp.dot(left[owner * tall : (owner + 1) * tall, :], right_ref[...], preferred_element_type=jnp.float32)

    @pl.when(step == pl.num_programs(0) - 1)
    def _():
        code_tiles(place_ref, acc, o_ref, nq=nq, blocks=blocks)


def lean_tiles(place, queries, beside, rows, *, cap, span, blocks, extra, per_step=8):
    nq = queries.shape[0]
    sources, depth, width = rows.shape
    lanes = blocks * width + LANES
    targets = 16 * HALVES
    deep_lanes = extra // 16 * width
    steps = sources // per_step
    far_at = deep_lanes // LANES
    grid_spec = pltpu.PrefetchScalarGridSpec(
        num_scalar_prefetch=1,
        grid=(sources // per_step,),
        in_specs=[
            pl.BlockSpec((nq, per_step * span), lambda i, _: (0, i)),
            pl.BlockSpec((per_step * 16, deep_lanes), lambda i, _: (steps - 1 - i, 0)),
            pl.BlockSpec((per_step * 16, LANES), lambda i, _: (steps - 1 - i, far_at)),
            pl.BlockSpec((per_step, depth, width), lambda i, _: (i, 0, 0)),
        ],
        out_specs=pl.BlockSpec((targets, nq // 16, lanes), lambda i, _: (0, 0, 0)),
        scratch_shapes=[
            pltpu.VMEM((HALVES * blocks * nq, per_step * (cap + extra)), jnp.bfloat16),
            pltpu.VMEM((HALVES, blocks * nq, width), jnp.float32),
            pltpu.VMEM((per_step * (cap + extra), width), jnp.bfloat16),
        ],
    )
    return pl.pallas_call(
        functools.partial(lean_kernel, cap=cap, span=span, per_step=per_step, blocks=blocks, extra=extra),
        grid_spec=grid_spec,
        out_shape=jax.ShapeDtypeStruct((targets, nq // 16, lanes), jnp.int16),
        compiler_params=pltpu.CompilerParams(vmem_limit_bytes=56 << 20),
        cost_estimate=pl.CostEstimate(
            flops=2 * nq * sources * HALVES * (cap + extra) * width * blocks,
            bytes_accessed=2 * (queries.size + rows.size),
            transcendentals=0,
        ),
        name="lean_tiles",
    )(place, queries, beside, beside, rows)


def gram_kernel(flip_ref, q_ref, x_ref, o_ref, left, acc, *, cap, span, per_step, blocks):
    step = pl.program_id(0)
    width = x_ref.shape[2]
    nq = q_ref.shape[0]
    pair_rows = 2 * cap
    for owner in range(HALVES):
        for pair in range(per_step // 2):
            docs, ids = [], []
            for k in range(2):
                base = HALVES * cap
                meta = x_ref[2 * pair + k, base : base + TILE, :][owner : owner + 1, :].astype(jnp.float32)
                docs.append(meta[:, :cap] + float(k * span))
                ids.append(meta[:, cap : 2 * cap])
            doc = jnp.concatenate(docs, axis=1).astype(jnp.int32)
            block = jnp.concatenate(ids, axis=1)
            rows = lax.broadcasted_iota(jnp.int32, (2 * span, pair_rows), 0)
            chosen = jnp.where(rows == doc, 1.0, 0.0).astype(jnp.bfloat16)
            queries = q_ref[:, pair * 2 * span : (pair + 1) * 2 * span]
            picked = jnp.dot(queries, chosen, preferred_element_type=jnp.float32).astype(jnp.bfloat16)
            for b in range(blocks):
                kept = picked * jnp.where(block == float(b), 1.0, 0.0).astype(jnp.bfloat16)
                left[owner, b * nq : (b + 1) * nq, pair * pair_rows : (pair + 1) * pair_rows] = kept
        right = jnp.concatenate([x_ref[k, owner * cap : (owner + 1) * cap, :] for k in range(per_step)], axis=0)
        product = jnp.dot(left[owner], right, preferred_element_type=jnp.float32)

        @pl.when(step == 0)
        def _():
            acc[owner] = product

        @pl.when(step > 0)
        def _():
            acc[owner] += product

    @pl.when(step == pl.num_programs(0) - 1)
    def _():
        code_tiles(flip_ref, acc, o_ref, nq=nq, blocks=blocks)


def partial_tiles(flip, queries, rows, *, cap, span, blocks, per_step=4):
    nq, docs = queries.shape
    sources, depth, width = rows.shape
    lanes = blocks * width + LANES
    targets = 16 * HALVES
    grid_spec = pltpu.PrefetchScalarGridSpec(
        num_scalar_prefetch=1,
        grid=(sources // per_step,),
        in_specs=[
            pl.BlockSpec((nq, per_step * span), lambda i, _: (0, i)),
            pl.BlockSpec((per_step, depth, width), lambda i, _: (i, 0, 0)),
        ],
        out_specs=pl.BlockSpec((targets, nq // 16, lanes), lambda i, _: (0, 0, 0)),
        scratch_shapes=[
            pltpu.VMEM((HALVES, blocks * nq, per_step * cap), jnp.bfloat16),
            pltpu.VMEM((HALVES, blocks * nq, width), jnp.float32),
        ],
    )
    return pl.pallas_call(
        functools.partial(gram_kernel, cap=cap, span=span, per_step=per_step, blocks=blocks),
        grid_spec=grid_spec,
        out_shape=jax.ShapeDtypeStruct((targets, nq // 16, lanes), jnp.int16),
        compiler_params=pltpu.CompilerParams(vmem_limit_bytes=48 << 20),
        cost_estimate=pl.CostEstimate(
            flops=2 * nq * sources * HALVES * cap * width * blocks,
            bytes_accessed=2 * (queries.size + rows.size),
            transcendentals=0,
        ),
        name="gram_tiles",
    )(flip, queries, rows)


def payload_kernel(counts_ref, first_ref, slots_ref, low_ref, high_ref, o_ref, *, shallow, blocks):
    step = pl.program_id(0)
    here, z_size = low_ref.shape[0], low_ref.shape[0] * pl.num_programs(0)
    lane = lax.broadcasted_iota(jnp.int32, (1, slots_ref.shape[1]), 1)
    base = HALVES * shallow
    beyond = jnp.int32(0)
    for owner in range(slots_ref.shape[0]):
        beyond += jnp.maximum(counts_ref[owner] - shallow, 0)
    crowded = jnp.where(beyond > EXTRA, 1.0, 0.0)
    for r in range(here):
        z = step * here + r
        docs, ids = [], []
        for half in range(HALVES):
            owner = half * z_size + z
            slots = slots_ref[pl.ds(owner, 1), :]
            doc = lax.shift_right_logical(slots, blocks.bit_length() - 1) - first_ref[0]
            docs.append(doc.astype(jnp.float32))
            ids.append(jnp.where(lane < counts_ref[owner], slots & (blocks - 1), DEAD).astype(jnp.float32))
        rest = jnp.full((TILE - 2, o_ref.shape[2]), crowded)
        meta = jnp.concatenate([jnp.concatenate(docs, axis=1), jnp.concatenate(ids, axis=1), rest], axis=0)
        o_ref[r, :shallow, :] = low_ref[r, :shallow, :]
        o_ref[r, shallow:base, :] = high_ref[r, :shallow, :]
        o_ref[r, base:, :] = meta.astype(jnp.bfloat16)


def payload(counts, first, slots, values, *, blocks, per_step=4):
    owners, cap, width = values.shape
    z_size = owners // HALVES
    depth = HALVES * SHALLOW + TILE
    steps = z_size // per_step
    grid_spec = pltpu.PrefetchScalarGridSpec(
        num_scalar_prefetch=2,
        grid=(steps,),
        in_specs=[
            pl.BlockSpec(slots.shape, lambda i, *_: (0, 0)),
            pl.BlockSpec((per_step, cap, width), lambda i, *_: (i, 0, 0)),
            pl.BlockSpec((per_step, cap, width), lambda i, *_: (i + steps, 0, 0)),
        ],
        out_specs=pl.BlockSpec((per_step, depth, width), lambda i, *_: (i, 0, 0)),
    )
    return pl.pallas_call(
        functools.partial(payload_kernel, shallow=SHALLOW, blocks=blocks),
        grid_spec=grid_spec,
        out_shape=jax.ShapeDtypeStruct((z_size, depth, width), jnp.bfloat16),
        compiler_params=pltpu.CompilerParams(vmem_limit_bytes=16 << 20),
        cost_estimate=pl.CostEstimate(flops=0, bytes_accessed=4 * values.size, transcendentals=0),
        name="payload",
    )(counts, first, slots, values, values)


def sum_kernel(p_ref, o_ref, *, blocks, width):
    groups = p_ref.shape[0]
    scale = jnp.exp2(p_ref[:, :, blocks * width :].astype(jnp.float32) * (1.0 / CODE_STEP))
    for b in range(blocks):
        total = jnp.zeros((p_ref.shape[1], width), jnp.float32)
        for g in range(groups):
            part = p_ref[g, :, b * width : (b + 1) * width].astype(jnp.float32)
            total = total + part * scale[g, :, b : b + 1]
        o_ref[:, b * width : (b + 1) * width] = total


def summed(parts, *, blocks, width):
    return pl.pallas_call(
        functools.partial(sum_kernel, blocks=blocks, width=width),
        out_shape=jax.ShapeDtypeStruct((parts.shape[1], blocks * width), jnp.float32),
        in_specs=[pl.BlockSpec(memory_space=pltpu.VMEM)],
        out_specs=pl.BlockSpec(memory_space=pltpu.VMEM),
        compiler_params=pltpu.CompilerParams(vmem_limit_bytes=16 << 20),
        name="sum_parts",
    )(parts)


def per_device(query_rows, row_values, row_slots, row_counts):
    z_size = lax.axis_size("z")
    owners = HALVES * z_size
    doc_count = query_rows.shape[1]
    span = doc_count // owners
    _, _, _, cap, width = row_values.shape
    blocks = 8
    y = lax.axis_index("y")
    me = y * z_size + lax.axis_index("z")

    slots = row_slots[0, 0]
    counts = row_counts[0, 0]
    sent = payload(counts, (me * span).reshape(1), slots, row_values[0, 0], blocks=blocks)
    rows = lax.all_to_all(sent, "z", split_axis=0, concat_axis=0, tiled=True)

    half_docs = doc_count // HALVES
    mine = lax.dynamic_slice_in_dim(query_rows, y * half_docs, half_docs, 1)
    theirs = lax.dynamic_slice_in_dim(query_rows, (1 - y) * half_docs, half_docs, 1)
    mirror = lax.ppermute(theirs, "y", [(0, 1), (1, 0)])
    queries = lax.all_gather(jnp.concatenate([mine, mirror], axis=0), "z", axis=0, tiled=True)

    live = jnp.arange(cap, dtype=jnp.int32)[None, :] < counts[:, None]
    doc = slots // blocks - me * span
    beyond = jnp.maximum(counts - SHALLOW, 0)
    order = jnp.arange(owners, dtype=jnp.int32)
    before = jnp.sum(jnp.where(order[None, :] < order[:, None], beyond[None, :], 0), axis=1)
    depth = cap - SHALLOW
    spot = jnp.where(live[:, SHALLOW:], before[:, None] + jnp.arange(depth, dtype=jnp.int32)[None, :], EXTRA)
    spot = spot.reshape(1, owners * depth)
    taken = spot == jnp.arange(EXTRA, dtype=jnp.int32)[:, None]
    deep = row_values[0, 0, :, SHALLOW:, :].reshape(owners * depth, width)
    deep = jnp.dot(taken.astype(jnp.bfloat16), deep, preferred_element_type=jnp.float32).astype(jnp.bfloat16)
    packed = 1 + doc * blocks + slots % blocks + order[:, None] * (span * blocks)
    packed = jnp.sum(jnp.where(taken, packed[:, SHALLOW:].reshape(1, owners * depth), 0), axis=1)
    code = jnp.maximum(packed - 1, 0)
    target = jnp.where(packed > 0, code // (span * blocks), DEAD)
    far = jnp.stack([code % (span * blocks) // blocks, code % blocks, target]).astype(jnp.bfloat16)
    far = jnp.pad(far, ((0, 16 - 3), (SHALLOW, LANES - SHALLOW - EXTRA)))
    beside = jnp.concatenate([deep[g : g + 16] for g in range(0, EXTRA, 16)] + [far], axis=1)
    downward = [list(range(z_size - 1, -1, -1))]
    beside = lax.all_gather(beside, "z", axis=0, tiled=True, axis_index_groups=downward)
    home = jnp.stack([y, lax.axis_index("z"), jnp.int32(z_size)]).astype(jnp.int32)

    def lean(place, queries, beside, rows, row_values):
        return lean_tiles(place, queries, beside, rows, cap=SHALLOW, span=span, blocks=blocks, extra=EXTRA)

    def full(place, queries, beside, rows, row_values):
        block = jnp.where(live, slots % blocks, DEAD)
        meta = jnp.concatenate([doc, block], axis=1).reshape(HALVES, z_size, 2 * cap).transpose(1, 0, 2)
        meta = jnp.pad(meta, ((0, 0), (0, TILE - HALVES), (0, 0))).astype(jnp.bfloat16)
        values = row_values[0, 0]
        sent = jnp.concatenate([values[:z_size], values[z_size:], meta], axis=1)
        rows = lax.all_to_all(sent, "z", split_axis=0, concat_axis=0, tiled=True)
        return partial_tiles(place, queries, rows, cap=cap, span=span, blocks=blocks)

    flags = rows[:, HALVES * SHALLOW + TILE - 1, 0].astype(jnp.float32)
    coded = lax.cond(jnp.max(flags) > 0.5, full, lean, home, queries, beside, rows, row_values)
    parts = lax.all_to_all(coded, ("doc", "y"), split_axis=0, concat_axis=0, tiled=True)
    return summed(parts, blocks=blocks, width=width)


def solution(mesh):
    docs, owners = mesh.devices.shape
    split = Mesh(mesh.devices.reshape(docs, HALVES, owners // HALVES), ("doc", "y", "z"))
    blk = ("y", "z")
    in_specs = (
        P(blk, "doc"),
        P("doc", blk, None, None, None),
        P("doc", blk, None, None),
        P("doc", blk, None),
    )
    return jax.shard_map(
        per_device, mesh=split, in_specs=in_specs, out_specs=P("doc", blk), check_vma=False
    )
```

```python
import functools

import jax
import jax.numpy as jnp
from jax import lax
from jax.experimental import pallas as pl
from jax.experimental.pallas import tpu as pltpu
from jax.sharding import Mesh
from jax.sharding import PartitionSpec as P

CORES = 2
HALVES = 2
CODE_STEP = 64.0
TOP = 32700.0
TINY = 2.0**-110
LANES = 128
TILE = 8
SHALLOW = 96
EXTRA = 32
DEAD = 64


def coded_rows(tiles, blocks):
    lane = lax.broadcasted_iota(jnp.int32, (16, LANES), 1)
    peaks = jnp.full((16, LANES), TINY, jnp.float32)
    for b in range(blocks):
        peak = jnp.max(jnp.abs(tiles(b)), axis=1, keepdims=True)
        peaks = jnp.where(lane == b, jnp.maximum(peak, TINY), peaks)
    code = jnp.ceil((jnp.log2(peaks) - jnp.log2(TOP)) * CODE_STEP)
    inverse = jnp.exp2(code * (-1.0 / CODE_STEP))
    out = [jnp.floor(tiles(b) * inverse[:, b : b + 1] + 0.5).astype(jnp.int32).astype(jnp.int16) for b in range(blocks)]
    return out, code.astype(jnp.int32).astype(jnp.int16)


def code_tiles(place_ref, acc, keep_ref, give_ref, *, nq, blocks):
    width = acc.shape[2]
    flip, core = place_ref[0], place_ref[3]
    half = nq // (2 * 16)

    def tile_of(owner, b, m, slot):
        base = pl.multiple_of(b * nq + m * 32 + slot * 8, 8)
        return jnp.concatenate([acc[owner, pl.ds(base, 8), :], acc[owner, pl.ds(base + 16, 8), :]], axis=0)

    for owner in range(HALVES):
        for pair in range(half // CORES):
            for slot in range(2):
                target = ((slot + flip - 2 * slot * flip) * (half // CORES) + pair) * HALVES + owner
                for b in range(blocks):
                    keep_ref[target, :, b * width : (b + 1) * width] = tile_of(owner, b, pair * CORES + core, slot)
                other = lambda b: tile_of(owner, b, pair * CORES + 1 - core, slot)
                out, code = coded_rows(other, blocks)
                for b in range(blocks):
                    give_ref[target, :, b * width : (b + 1) * width] = out[b]
                give_ref[target, :, blocks * width :] = code


def merge_kernel(keep_ref, got_ref, o_ref, *, blocks):
    width = keep_ref.shape[2] // blocks
    for t in range(keep_ref.shape[0]):
        scale = jnp.exp2(got_ref[t, :, blocks * width :].astype(jnp.float32) * (1.0 / CODE_STEP))

        def total(b):
            lanes = slice(b * width, (b + 1) * width)
            return keep_ref[t, :, lanes] + got_ref[t, :, lanes].astype(jnp.float32) * scale[:, b : b + 1]

        sums = [total(b) for b in range(blocks)]
        out, code = coded_rows(lambda b: sums[b], blocks)
        for b in range(blocks):
            o_ref[t, :, b * width : (b + 1) * width] = out[b]
        o_ref[t, :, blocks * width :] = code


def merged(keep, got, *, blocks, per_step=4):
    targets, rows, lanes = got.shape
    return pl.pallas_call(
        functools.partial(merge_kernel, blocks=blocks),
        grid=(targets // per_step,),
        in_specs=[
            pl.BlockSpec((per_step, rows, keep.shape[2]), lambda i: (i, 0, 0)),
            pl.BlockSpec((per_step, rows, lanes), lambda i: (i, 0, 0)),
        ],
        out_specs=pl.BlockSpec((per_step, rows, lanes), lambda i: (i, 0, 0)),
        out_shape=jax.ShapeDtypeStruct(got.shape, jnp.int16),
        compiler_params=pltpu.CompilerParams(vmem_limit_bytes=16 << 20),
        name="merge",
    )(keep, got)


def lean_kernel(place_ref, q_ref, deep_ref, far_ref, x_ref, keep_ref, give_ref, left, acc, right_ref, *, cap, span, per_step, blocks, extra):
    step = pl.program_id(0)
    width = x_ref.shape[2]
    nq = q_ref.shape[0]
    base = HALVES * cap
    window = 2 * LANES
    tall = blocks * nq
    lane = lax.broadcasted_iota(jnp.int32, (1, LANES), 1)

    @pl.when(step == 0)
    def _():
        acc[...] = jnp.zeros_like(acc)

    places = lax.broadcasted_iota(jnp.int32, (window, window), 0)
    got, codes_of = [], []
    for k in range(per_step):
        meta = x_ref[k, base : base + TILE, :].astype(jnp.float32)
        behind = (per_step - 1 - k) * 16
        far = far_ref[behind : behind + TILE, :].astype(jnp.float32)
        docs, ids = [], []
        for owner in range(HALVES):
            lanes = slice(owner * LANES, (owner + 1) * LANES)
            to_owner = far[2:3, :] == (place_ref[1] + owner * place_ref[2]).astype(jnp.float32)
            docs.append(jnp.where(lane < cap, meta[0:1, lanes], far[0:1, :]))
            ids.append(jnp.where(lane < cap, meta[1:2, lanes], jnp.where(to_owner, far[1:2, :], float(DEAD))))
        start = k * span // LANES * LANES
        doc = jnp.concatenate(docs, axis=1).astype(jnp.int32) + (k * span - start)
        chosen = jnp.where(places == doc, 1.0, 0.0).astype(jnp.bfloat16)
        queries = q_ref[:, start : start + window]
        picked = jnp.dot(queries, chosen, preferred_element_type=jnp.float32).astype(jnp.bfloat16)
        got.append(picked)
        codes_of.append(ids)
    for owner in range(HALVES):
        lanes = slice(owner * LANES, (owner + 1) * LANES)
        for k in range(per_step):
            for b in range(blocks):
                kept = got[k][:, lanes] * jnp.where(codes_of[k][owner] == float(b), 1.0, 0.0).astype(jnp.bfloat16)
                left[owner * tall + b * nq : owner * tall + (b + 1) * nq, k * LANES : (k + 1) * LANES] = kept
        right = []
        for k in range(per_step):
            right.append(x_ref[k, owner * cap : (owner + 1) * cap, :])
            behind = (per_step - 1 - k) * 16
            right += [deep_ref[behind : behind + 16, g * width : (g + 1) * width] for g in range(extra // 16)]
        right = jnp.concatenate(right, axis=0)
        right_ref[...] = right
        acc[owner] += jnp.dot(left[owner * tall : (owner + 1) * tall, :], right_ref[...], preferred_element_type=jnp.float32)

    @pl.when(step == pl.num_programs(0) - 1)
    def _():
        code_tiles(place_ref, acc, keep_ref, give_ref, nq=nq, blocks=blocks)


def lean_tiles(place, queries, beside, rows, *, cap, span, blocks, extra, per_step=4):
    nq = queries.shape[0]
    sources, depth, width = rows.shape
    lanes = blocks * width + LANES
    targets = 16 // CORES * HALVES
    deep_lanes = extra // 16 * width
    steps = sources // per_step
    far_at = deep_lanes // LANES
    grid_spec = pltpu.PrefetchScalarGridSpec(
        num_scalar_prefetch=1,
        grid=(sources // per_step,),
        in_specs=[
            pl.BlockSpec((nq, per_step * span), lambda i, _: (0, i)),
            pl.BlockSpec((per_step * 16, deep_lanes), lambda i, _: (steps - 1 - i, 0)),
            pl.BlockSpec((per_step * 16, LANES), lambda i, _: (steps - 1 - i, far_at)),
            pl.BlockSpec((per_step, depth, width), lambda i, _: (i, 0, 0)),
        ],
        out_specs=[
            pl.BlockSpec((targets, nq // 16, blocks * width), lambda i, _: (0, 0, 0)),
            pl.BlockSpec((targets, nq // 16, lanes), lambda i, _: (0, 0, 0)),
        ],
        scratch_shapes=[
            pltpu.VMEM((HALVES * blocks * nq, per_step * (cap + extra)), jnp.bfloat16),
            pltpu.VMEM((HALVES, blocks * nq, width), jnp.float32),
            pltpu.VMEM((per_step * (cap + extra), width), jnp.bfloat16),
        ],
    )
    return pl.pallas_call(
        functools.partial(lean_kernel, cap=cap, span=span, per_step=per_step, blocks=blocks, extra=extra),
        grid_spec=grid_spec,
        out_shape=[
            jax.ShapeDtypeStruct((targets, nq // 16, blocks * width), jnp.float32),
            jax.ShapeDtypeStruct((targets, nq // 16, lanes), jnp.int16),
        ],
        compiler_params=pltpu.CompilerParams(vmem_limit_bytes=56 << 20),
        cost_estimate=pl.CostEstimate(
            flops=2 * nq * sources * HALVES * (cap + extra) * width * blocks,
            bytes_accessed=2 * (queries.size + rows.size),
            transcendentals=0,
        ),
        name="lean_tiles",
    )(place, queries, beside, beside, rows)


def gram_kernel(place_ref, q_ref, x_ref, keep_ref, give_ref, left, acc, *, cap, span, per_step, blocks):
    step = pl.program_id(0)
    width = x_ref.shape[2]
    nq = q_ref.shape[0]
    pair_rows = 2 * cap
    for owner in range(HALVES):
        for pair in range(per_step // 2):
            docs, ids = [], []
            for k in range(2):
                base = HALVES * cap
                meta = x_ref[2 * pair + k, base : base + TILE, :][owner : owner + 1, :].astype(jnp.float32)
                docs.append(meta[:, :cap] + float(k * span))
                ids.append(meta[:, cap : 2 * cap])
            doc = jnp.concatenate(docs, axis=1).astype(jnp.int32)
            block = jnp.concatenate(ids, axis=1)
            rows = lax.broadcasted_iota(jnp.int32, (2 * span, pair_rows), 0)
            chosen = jnp.where(rows == doc, 1.0, 0.0).astype(jnp.bfloat16)
            queries = q_ref[:, pair * 2 * span : (pair + 1) * 2 * span]
            picked = jnp.dot(queries, chosen, preferred_element_type=jnp.float32).astype(jnp.bfloat16)
            for b in range(blocks):
                kept = picked * jnp.where(block == float(b), 1.0, 0.0).astype(jnp.bfloat16)
                left[owner, b * nq : (b + 1) * nq, pair * pair_rows : (pair + 1) * pair_rows] = kept
        right = jnp.concatenate([x_ref[k, owner * cap : (owner + 1) * cap, :] for k in range(per_step)], axis=0)
        product = jnp.dot(left[owner], right, preferred_element_type=jnp.float32)

        @pl.when(step == 0)
        def _():
            acc[owner] = product

        @pl.when(step > 0)
        def _():
            acc[owner] += product

    @pl.when(step == pl.num_programs(0) - 1)
    def _():
        code_tiles(place_ref, acc, keep_ref, give_ref, nq=nq, blocks=blocks)


def partial_tiles(flip, queries, rows, *, cap, span, blocks, per_step=4):
    nq, docs = queries.shape
    sources, depth, width = rows.shape
    lanes = blocks * width + LANES
    targets = 16 // CORES * HALVES
    grid_spec = pltpu.PrefetchScalarGridSpec(
        num_scalar_prefetch=1,
        grid=(sources // per_step,),
        in_specs=[
            pl.BlockSpec((nq, per_step * span), lambda i, _: (0, i)),
            pl.BlockSpec((per_step, depth, width), lambda i, _: (i, 0, 0)),
        ],
        out_specs=[
            pl.BlockSpec((targets, nq // 16, blocks * width), lambda i, _: (0, 0, 0)),
            pl.BlockSpec((targets, nq // 16, lanes), lambda i, _: (0, 0, 0)),
        ],
        scratch_shapes=[
            pltpu.VMEM((HALVES, blocks * nq, per_step * cap), jnp.bfloat16),
            pltpu.VMEM((HALVES, blocks * nq, width), jnp.float32),
        ],
    )
    return pl.pallas_call(
        functools.partial(gram_kernel, cap=cap, span=span, per_step=per_step, blocks=blocks),
        grid_spec=grid_spec,
        out_shape=[
            jax.ShapeDtypeStruct((targets, nq // 16, blocks * width), jnp.float32),
            jax.ShapeDtypeStruct((targets, nq // 16, lanes), jnp.int16),
        ],
        compiler_params=pltpu.CompilerParams(vmem_limit_bytes=48 << 20),
        cost_estimate=pl.CostEstimate(
            flops=2 * nq * sources * HALVES * cap * width * blocks,
            bytes_accessed=2 * (queries.size + rows.size),
            transcendentals=0,
        ),
        name="gram_tiles",
    )(flip, queries, rows)


def payload_kernel(counts_ref, first_ref, slots_ref, low_ref, high_ref, o_ref, *, shallow, blocks):
    step = pl.program_id(0)
    here, z_size = low_ref.shape[0], low_ref.shape[0] * pl.num_programs(0)
    lane = lax.broadcasted_iota(jnp.int32, (1, slots_ref.shape[1]), 1)
    base = HALVES * shallow
    beyond = jnp.int32(0)
    for owner in range(slots_ref.shape[0]):
        beyond += jnp.maximum(counts_ref[owner] - shallow, 0)
    crowded = jnp.where(beyond > EXTRA, 1.0, 0.0)
    for r in range(here):
        z = step * here + r
        docs, ids = [], []
        for half in range(HALVES):
            owner = half * z_size + z
            slots = slots_ref[pl.ds(owner, 1), :]
            doc = lax.shift_right_logical(slots, blocks.bit_length() - 1) - first_ref[0]
            docs.append(doc.astype(jnp.float32))
            ids.append(jnp.where(lane < counts_ref[owner], slots & (blocks - 1), DEAD).astype(jnp.float32))
        rest = jnp.full((TILE - 2, o_ref.shape[2]), crowded)
        meta = jnp.concatenate([jnp.concatenate(docs, axis=1), jnp.concatenate(ids, axis=1), rest], axis=0)
        o_ref[r, :shallow, :] = low_ref[r, :shallow, :]
        o_ref[r, shallow:base, :] = high_ref[r, :shallow, :]
        o_ref[r, base:, :] = meta.astype(jnp.bfloat16)


def payload(counts, first, slots, values, *, blocks, per_step=4):
    owners, cap, width = values.shape
    z_size = owners // HALVES
    depth = HALVES * SHALLOW + TILE
    steps = z_size // per_step
    grid_spec = pltpu.PrefetchScalarGridSpec(
        num_scalar_prefetch=2,
        grid=(steps,),
        in_specs=[
            pl.BlockSpec(slots.shape, lambda i, *_: (0, 0)),
            pl.BlockSpec((per_step, cap, width), lambda i, *_: (i, 0, 0)),
            pl.BlockSpec((per_step, cap, width), lambda i, *_: (i + steps, 0, 0)),
        ],
        out_specs=pl.BlockSpec((per_step, depth, width), lambda i, *_: (i, 0, 0)),
    )
    return pl.pallas_call(
        functools.partial(payload_kernel, shallow=SHALLOW, blocks=blocks),
        grid_spec=grid_spec,
        out_shape=jax.ShapeDtypeStruct((z_size, depth, width), jnp.bfloat16),
        compiler_params=pltpu.CompilerParams(vmem_limit_bytes=16 << 20),
        cost_estimate=pl.CostEstimate(flops=0, bytes_accessed=4 * values.size, transcendentals=0),
        name="payload",
    )(counts, first, slots, values, values)


def sum_kernel(p_ref, o_ref, *, blocks, width):
    groups = p_ref.shape[0]
    scale = jnp.exp2(p_ref[:, :, blocks * width :].astype(jnp.float32) * (1.0 / CODE_STEP))
    for b in range(blocks):
        total = jnp.zeros((p_ref.shape[1], width), jnp.float32)
        for g in range(groups):
            part = p_ref[g, :, b * width : (b + 1) * width].astype(jnp.float32)
            total = total + part * scale[g, :, b : b + 1]
        o_ref[:, b * width : (b + 1) * width] = total


def summed(parts, *, blocks, width):
    return pl.pallas_call(
        functools.partial(sum_kernel, blocks=blocks, width=width),
        out_shape=jax.ShapeDtypeStruct((parts.shape[1], blocks * width), jnp.float32),
        in_specs=[pl.BlockSpec(memory_space=pltpu.VMEM)],
        out_specs=pl.BlockSpec(memory_space=pltpu.VMEM),
        compiler_params=pltpu.CompilerParams(vmem_limit_bytes=16 << 20),
        name="sum_parts",
    )(parts)


def per_device(query_rows, row_values, row_slots, row_counts):
    z_size = lax.axis_size("z")
    owners = HALVES * z_size
    doc_count = query_rows.shape[1]
    span = doc_count // owners
    _, _, _, cap, width = row_values.shape
    blocks = 8
    y = lax.axis_index("y")
    me = y * z_size + lax.axis_index("z")

    slots = row_slots[0, 0]
    counts = row_counts[0, 0]
    sent = payload(counts, (me * span).reshape(1), slots, row_values[0, 0], blocks=blocks)
    rows = lax.all_to_all(sent, "z", split_axis=0, concat_axis=0, tiled=True)

    half_docs = doc_count // HALVES
    mine = lax.dynamic_slice_in_dim(query_rows, y * half_docs, half_docs, 1)
    theirs = lax.dynamic_slice_in_dim(query_rows, (1 - y) * half_docs, half_docs, 1)
    mirror = lax.ppermute(theirs, "y", [(0, 1), (1, 0)])
    queries = lax.all_gather(jnp.concatenate([mine, mirror], axis=0), "z", axis=0, tiled=True)

    live = jnp.arange(cap, dtype=jnp.int32)[None, :] < counts[:, None]
    doc = slots // blocks - me * span
    beyond = jnp.maximum(counts - SHALLOW, 0)
    order = jnp.arange(owners, dtype=jnp.int32)
    before = jnp.sum(jnp.where(order[None, :] < order[:, None], beyond[None, :], 0), axis=1)
    depth = cap - SHALLOW
    spot = jnp.where(live[:, SHALLOW:], before[:, None] + jnp.arange(depth, dtype=jnp.int32)[None, :], EXTRA)
    spot = spot.reshape(1, owners * depth)
    taken = spot == jnp.arange(EXTRA, dtype=jnp.int32)[:, None]
    deep = row_values[0, 0, :, SHALLOW:, :].reshape(owners * depth, width)
    deep = jnp.dot(taken.astype(jnp.bfloat16), deep, preferred_element_type=jnp.float32).astype(jnp.bfloat16)
    packed = 1 + doc * blocks + slots % blocks + order[:, None] * (span * blocks)
    packed = jnp.sum(jnp.where(taken, packed[:, SHALLOW:].reshape(1, owners * depth), 0), axis=1)
    code = jnp.maximum(packed - 1, 0)
    target = jnp.where(packed > 0, code // (span * blocks), DEAD)
    far = jnp.stack([code % (span * blocks) // blocks, code % blocks, target]).astype(jnp.bfloat16)
    far = jnp.pad(far, ((0, 16 - 3), (SHALLOW, LANES - SHALLOW - EXTRA)))
    beside = jnp.concatenate([deep[g : g + 16] for g in range(0, EXTRA, 16)] + [far], axis=1)
    downward = [list(range(z_size - 1, -1, -1))]
    beside = lax.all_gather(beside, "z", axis=0, tiled=True, axis_index_groups=downward)
    home = jnp.stack([y, lax.axis_index("z"), jnp.int32(z_size), lax.axis_index("core")]).astype(jnp.int32)

    def lean(place, queries, beside, rows, row_values):
        return lean_tiles(place, queries, beside, rows, cap=SHALLOW, span=span, blocks=blocks, extra=EXTRA)

    def full(place, queries, beside, rows, row_values):
        block = jnp.where(live, slots % blocks, DEAD)
        meta = jnp.concatenate([doc, block], axis=1).reshape(HALVES, z_size, 2 * cap).transpose(1, 0, 2)
        meta = jnp.pad(meta, ((0, 0), (0, TILE - HALVES), (0, 0))).astype(jnp.bfloat16)
        values = row_values[0, 0]
        sent = jnp.concatenate([values[:z_size], values[z_size:], meta], axis=1)
        rows = lax.all_to_all(sent, "z", split_axis=0, concat_axis=0, tiled=True)
        return partial_tiles(place, queries, rows, cap=cap, span=span, blocks=blocks)

    flags = rows[:, HALVES * SHALLOW + TILE - 1, 0].astype(jnp.float32)
    keep, give = lax.cond(jnp.max(flags) > 0.5, full, lean, home, queries, beside, rows, row_values)
    got = lax.ppermute(give, "core", [(0, 1), (1, 0)])
    coded = merged(keep, got, blocks=blocks)
    parts = lax.all_to_all(coded, ("chip", "y"), split_axis=0, concat_axis=0, tiled=True)
    return summed(parts, blocks=blocks, width=width)


def solution(mesh):
    docs, owners = mesh.devices.shape
    shape = (docs // CORES, CORES, HALVES, owners // HALVES)
    split = Mesh(mesh.devices.reshape(shape), ("chip", "core", "y", "z"))
    doc, blk = ("chip", "core"), ("y", "z")
    in_specs = (
        P(blk, doc),
        P(doc, blk, None, None, None),
        P(doc, blk, None, None),
        P(doc, blk, None),
    )
    return jax.shard_map(
        per_device, mesh=split, in_specs=in_specs, out_specs=P(doc, blk), check_vma=False
    )
```

```python
import functools

import jax
import jax.numpy as jnp
from jax import lax
from jax.experimental import pallas as pl
from jax.experimental.pallas import tpu as pltpu
from jax.sharding import Mesh
from jax.sharding import PartitionSpec as P

CORES = 2
HALVES = 2
CODE_STEP = 64.0
TOP = 32700.0
TINY = 2.0**-110
LANES = 128
TILE = 8
SHALLOW = 96
EXTRA = 32
DEAD = 64


def coded_rows(tiles, blocks):
    lane = lax.broadcasted_iota(jnp.int32, (16, LANES), 1)
    peaks = jnp.full((16, LANES), TINY, jnp.float32)
    for b in range(blocks):
        peak = jnp.max(jnp.abs(tiles(b)), axis=1, keepdims=True)
        peaks = jnp.where(lane == b, jnp.maximum(peak, TINY), peaks)
    code = jnp.ceil((jnp.log2(peaks) - jnp.log2(TOP)) * CODE_STEP)
    inverse = jnp.exp2(code * (-1.0 / CODE_STEP))
    out = [jnp.floor(tiles(b) * inverse[:, b : b + 1] + 0.5).astype(jnp.int32).astype(jnp.int16) for b in range(blocks)]
    return out, code.astype(jnp.int32).astype(jnp.int16)


def code_tiles(place_ref, acc, keep_ref, give_ref, *, nq, blocks):
    width = acc.shape[2]
    flip, core = place_ref[0], place_ref[3]
    half = nq // (2 * 16)

    def tile_of(owner, b, m, slot):
        base = pl.multiple_of(b * nq + m * 32 + slot * 8, 8)
        return jnp.concatenate([acc[owner, pl.ds(base, 8), :], acc[owner, pl.ds(base + 16, 8), :]], axis=0)

    for owner in range(HALVES):
        for pair in range(half // CORES):
            for slot in range(2):
                target = ((slot + flip - 2 * slot * flip) * (half // CORES) + pair) * HALVES + owner
                for b in range(blocks):
                    keep_ref[target, :, b * width : (b + 1) * width] = tile_of(owner, b, pair * CORES + core, slot)
                other = lambda b: tile_of(owner, b, pair * CORES + 1 - core, slot)
                out, code = coded_rows(other, blocks)
                for b in range(blocks):
                    give_ref[target, :, b * width : (b + 1) * width] = out[b]
                give_ref[target, :, blocks * width :] = code


def merge_kernel(keep_ref, got_ref, o_ref, *, blocks):
    width = keep_ref.shape[2] // blocks
    for t in range(keep_ref.shape[0]):
        scale = jnp.exp2(got_ref[t, :, blocks * width :].astype(jnp.float32) * (1.0 / CODE_STEP))

        def total(b):
            lanes = slice(b * width, (b + 1) * width)
            return keep_ref[t, :, lanes] + got_ref[t, :, lanes].astype(jnp.float32) * scale[:, b : b + 1]

        sums = [total(b) for b in range(blocks)]
        out, code = coded_rows(lambda b: sums[b], blocks)
        for b in range(blocks):
            o_ref[t, :, b * width : (b + 1) * width] = out[b]
        o_ref[t, :, blocks * width :] = code


def merged(keep, got, *, blocks, per_step=4):
    targets, rows, lanes = got.shape
    return pl.pallas_call(
        functools.partial(merge_kernel, blocks=blocks),
        grid=(targets // per_step,),
        in_specs=[
            pl.BlockSpec((per_step, rows, keep.shape[2]), lambda i: (i, 0, 0)),
            pl.BlockSpec((per_step, rows, lanes), lambda i: (i, 0, 0)),
        ],
        out_specs=pl.BlockSpec((per_step, rows, lanes), lambda i: (i, 0, 0)),
        out_shape=jax.ShapeDtypeStruct(got.shape, jnp.int16),
        compiler_params=pltpu.CompilerParams(vmem_limit_bytes=16 << 20),
        name="merge",
    )(keep, got)


def lean_kernel(place_ref, q_ref, deep_ref, far_ref, x_ref, keep_ref, give_ref, left, acc, right_ref, *, cap, span, per_step, blocks, extra):
    step = pl.program_id(0)
    width = x_ref.shape[2]
    nq = q_ref.shape[0]
    base = HALVES * cap
    window = 2 * LANES
    tall = blocks * nq
    lane = lax.broadcasted_iota(jnp.int32, (1, LANES), 1)

    @pl.when(step == 0)
    def _():
        acc[...] = jnp.zeros_like(acc)

    places = lax.broadcasted_iota(jnp.int32, (window, window), 0)
    got, codes_of = [], []
    for k in range(per_step):
        meta = x_ref[k, base : base + TILE, :].astype(jnp.float32)
        behind = (per_step - 1 - k) * 16
        far = far_ref[behind : behind + TILE, :].astype(jnp.float32)
        docs, ids = [], []
        for owner in range(HALVES):
            lanes = slice(owner * LANES, (owner + 1) * LANES)
            to_owner = far[2:3, :] == (place_ref[1] + owner * place_ref[2]).astype(jnp.float32)
            docs.append(jnp.where(lane < cap, meta[0:1, lanes], far[0:1, :]))
            ids.append(jnp.where(lane < cap, meta[1:2, lanes], jnp.where(to_owner, far[1:2, :], float(DEAD))))
        start = k * span // LANES * LANES
        doc = jnp.concatenate(docs, axis=1).astype(jnp.int32) + (k * span - start)
        chosen = jnp.where(places == doc, 1.0, 0.0).astype(jnp.bfloat16)
        queries = q_ref[:, start : start + window]
        picked = jnp.dot(queries, chosen, preferred_element_type=jnp.float32).astype(jnp.bfloat16)
        got.append(picked)
        codes_of.append(ids)
    for owner in range(HALVES):
        lanes = slice(owner * LANES, (owner + 1) * LANES)
        for k in range(per_step):
            for b in range(blocks):
                kept = got[k][:, lanes] * jnp.where(codes_of[k][owner] == float(b), 1.0, 0.0).astype(jnp.bfloat16)
                left[owner * tall + b * nq : owner * tall + (b + 1) * nq, k * LANES : (k + 1) * LANES] = kept
        right = []
        for k in range(per_step):
            right.append(x_ref[k, owner * cap : (owner + 1) * cap, :])
            behind = (per_step - 1 - k) * 16
            right += [deep_ref[behind : behind + 16, g * width : (g + 1) * width] for g in range(extra // 16)]
        right = jnp.concatenate(right, axis=0)
        right_ref[...] = right
        acc[owner] += jnp.dot(left[owner * tall : (owner + 1) * tall, :], right_ref[...], preferred_element_type=jnp.float32)

    @pl.when(step == pl.num_programs(0) - 1)
    def _():
        code_tiles(place_ref, acc, keep_ref, give_ref, nq=nq, blocks=blocks)


def lean_tiles(place, queries, beside, rows, *, cap, span, blocks, extra, per_step=4):
    nq = queries.shape[0]
    sources, depth, width = rows.shape
    lanes = blocks * width + LANES
    targets = 16 // CORES * HALVES
    deep_lanes = extra // 16 * width
    steps = sources // per_step
    far_at = deep_lanes // LANES
    grid_spec = pltpu.PrefetchScalarGridSpec(
        num_scalar_prefetch=1,
        grid=(sources // per_step,),
        in_specs=[
            pl.BlockSpec((nq, per_step * span), lambda i, _: (0, i)),
            pl.BlockSpec((per_step * 16, deep_lanes), lambda i, _: (steps - 1 - i, 0)),
            pl.BlockSpec((per_step * 16, LANES), lambda i, _: (steps - 1 - i, far_at)),
            pl.BlockSpec((per_step, depth, width), lambda i, _: (i, 0, 0)),
        ],
        out_specs=[
            pl.BlockSpec((targets, nq // 16, blocks * width), lambda i, _: (0, 0, 0)),
            pl.BlockSpec((targets, nq // 16, lanes), lambda i, _: (0, 0, 0)),
        ],
        scratch_shapes=[
            pltpu.VMEM((HALVES * blocks * nq, per_step * (cap + extra)), jnp.bfloat16),
            pltpu.VMEM((HALVES, blocks * nq, width), jnp.float32),
            pltpu.VMEM((per_step * (cap + extra), width), jnp.bfloat16),
        ],
    )
    return pl.pallas_call(
        functools.partial(lean_kernel, cap=cap, span=span, per_step=per_step, blocks=blocks, extra=extra),
        grid_spec=grid_spec,
        out_shape=[
            jax.ShapeDtypeStruct((targets, nq // 16, blocks * width), jnp.float32),
            jax.ShapeDtypeStruct((targets, nq // 16, lanes), jnp.int16),
        ],
        compiler_params=pltpu.CompilerParams(vmem_limit_bytes=56 << 20),
        cost_estimate=pl.CostEstimate(
            flops=2 * nq * sources * HALVES * (cap + extra) * width * blocks,
            bytes_accessed=2 * (queries.size + rows.size),
            transcendentals=0,
        ),
        name="lean_tiles",
    )(place, queries, beside, beside, rows)


def gram_kernel(place_ref, q_ref, x_ref, keep_ref, give_ref, left, acc, *, cap, span, per_step, blocks):
    step = pl.program_id(0)
    width = x_ref.shape[2]
    nq = q_ref.shape[0]
    pair_rows = 2 * cap
    for owner in range(HALVES):
        for pair in range(per_step // 2):
            docs, ids = [], []
            for k in range(2):
                base = HALVES * cap
                meta = x_ref[2 * pair + k, base : base + TILE, :][owner : owner + 1, :].astype(jnp.float32)
                docs.append(meta[:, :cap] + float(k * span))
                ids.append(meta[:, cap : 2 * cap])
            doc = jnp.concatenate(docs, axis=1).astype(jnp.int32)
            block = jnp.concatenate(ids, axis=1)
            rows = lax.broadcasted_iota(jnp.int32, (2 * span, pair_rows), 0)
            chosen = jnp.where(rows == doc, 1.0, 0.0).astype(jnp.bfloat16)
            queries = q_ref[:, pair * 2 * span : (pair + 1) * 2 * span]
            picked = jnp.dot(queries, chosen, preferred_element_type=jnp.float32).astype(jnp.bfloat16)
            for b in range(blocks):
                kept = picked * jnp.where(block == float(b), 1.0, 0.0).astype(jnp.bfloat16)
                left[owner, b * nq : (b + 1) * nq, pair * pair_rows : (pair + 1) * pair_rows] = kept
        right = jnp.concatenate([x_ref[k, owner * cap : (owner + 1) * cap, :] for k in range(per_step)], axis=0)
        product = jnp.dot(left[owner], right, preferred_element_type=jnp.float32)

        @pl.when(step == 0)
        def _():
            acc[owner] = product

        @pl.when(step > 0)
        def _():
            acc[owner] += product

    @pl.when(step == pl.num_programs(0) - 1)
    def _():
        code_tiles(place_ref, acc, keep_ref, give_ref, nq=nq, blocks=blocks)


def partial_tiles(flip, queries, rows, *, cap, span, blocks, per_step=4):
    nq, docs = queries.shape
    sources, depth, width = rows.shape
    lanes = blocks * width + LANES
    targets = 16 // CORES * HALVES
    grid_spec = pltpu.PrefetchScalarGridSpec(
        num_scalar_prefetch=1,
        grid=(sources // per_step,),
        in_specs=[
            pl.BlockSpec((nq, per_step * span), lambda i, _: (0, i)),
            pl.BlockSpec((per_step, depth, width), lambda i, _: (i, 0, 0)),
        ],
        out_specs=[
            pl.BlockSpec((targets, nq // 16, blocks * width), lambda i, _: (0, 0, 0)),
            pl.BlockSpec((targets, nq // 16, lanes), lambda i, _: (0, 0, 0)),
        ],
        scratch_shapes=[
            pltpu.VMEM((HALVES, blocks * nq, per_step * cap), jnp.bfloat16),
            pltpu.VMEM((HALVES, blocks * nq, width), jnp.float32),
        ],
    )
    return pl.pallas_call(
        functools.partial(gram_kernel, cap=cap, span=span, per_step=per_step, blocks=blocks),
        grid_spec=grid_spec,
        out_shape=[
            jax.ShapeDtypeStruct((targets, nq // 16, blocks * width), jnp.float32),
            jax.ShapeDtypeStruct((targets, nq // 16, lanes), jnp.int16),
        ],
        compiler_params=pltpu.CompilerParams(vmem_limit_bytes=48 << 20),
        cost_estimate=pl.CostEstimate(
            flops=2 * nq * sources * HALVES * cap * width * blocks,
            bytes_accessed=2 * (queries.size + rows.size),
            transcendentals=0,
        ),
        name="gram_tiles",
    )(flip, queries, rows)


def payload_kernel(counts_ref, first_ref, slots_ref, low_ref, high_ref, o_ref, *, shallow, blocks):
    step = pl.program_id(0)
    here, z_size = low_ref.shape[0], low_ref.shape[0] * pl.num_programs(0)
    lane = lax.broadcasted_iota(jnp.int32, (1, slots_ref.shape[1]), 1)
    base = HALVES * shallow
    beyond = jnp.int32(0)
    for owner in range(slots_ref.shape[0]):
        beyond += jnp.maximum(counts_ref[owner] - shallow, 0)
    crowded = jnp.where(beyond > EXTRA, 1.0, 0.0)
    for r in range(here):
        z = step * here + r
        docs, ids = [], []
        for half in range(HALVES):
            owner = half * z_size + z
            slots = slots_ref[pl.ds(owner, 1), :]
            doc = lax.shift_right_logical(slots, blocks.bit_length() - 1) - first_ref[0]
            docs.append(doc.astype(jnp.float32))
            ids.append(jnp.where(lane < counts_ref[owner], slots & (blocks - 1), DEAD).astype(jnp.float32))
        rest = jnp.full((TILE - 2, o_ref.shape[2]), crowded)
        meta = jnp.concatenate([jnp.concatenate(docs, axis=1), jnp.concatenate(ids, axis=1), rest], axis=0)
        o_ref[r, :shallow, :] = low_ref[r, :shallow, :]
        o_ref[r, shallow:base, :] = high_ref[r, :shallow, :]
        o_ref[r, base:, :] = meta.astype(jnp.bfloat16)


def payload(counts, first, slots, values, *, blocks, per_step=8):
    owners, cap, width = values.shape
    z_size = owners // HALVES
    depth = HALVES * SHALLOW + TILE
    steps = z_size // per_step
    grid_spec = pltpu.PrefetchScalarGridSpec(
        num_scalar_prefetch=2,
        grid=(steps,),
        in_specs=[
            pl.BlockSpec(slots.shape, lambda i, *_: (0, 0)),
            pl.BlockSpec((per_step, SHALLOW, width), lambda i, *_: (i, 0, 0)),
            pl.BlockSpec((per_step, SHALLOW, width), lambda i, *_: (i + steps, 0, 0)),
        ],
        out_specs=pl.BlockSpec((per_step, depth, width), lambda i, *_: (i, 0, 0)),
    )
    return pl.pallas_call(
        functools.partial(payload_kernel, shallow=SHALLOW, blocks=blocks),
        grid_spec=grid_spec,
        out_shape=jax.ShapeDtypeStruct((z_size, depth, width), jnp.bfloat16),
        compiler_params=pltpu.CompilerParams(vmem_limit_bytes=16 << 20),
        cost_estimate=pl.CostEstimate(flops=0, bytes_accessed=4 * values.size, transcendentals=0),
        name="payload",
    )(counts, first, slots, values, values)


def sum_kernel(p_ref, o_ref, *, blocks, width):
    groups = p_ref.shape[0]
    scale = jnp.exp2(p_ref[:, :, blocks * width :].astype(jnp.float32) * (1.0 / CODE_STEP))
    for b in range(blocks):
        total = jnp.zeros((p_ref.shape[1], width), jnp.float32)
        for g in range(groups):
            part = p_ref[g, :, b * width : (b + 1) * width].astype(jnp.float32)
            total = total + part * scale[g, :, b : b + 1]
        o_ref[:, b * width : (b + 1) * width] = total


def summed(parts, *, blocks, width):
    return pl.pallas_call(
        functools.partial(sum_kernel, blocks=blocks, width=width),
        out_shape=jax.ShapeDtypeStruct((parts.shape[1], blocks * width), jnp.float32),
        in_specs=[pl.BlockSpec(memory_space=pltpu.VMEM)],
        out_specs=pl.BlockSpec(memory_space=pltpu.VMEM),
        compiler_params=pltpu.CompilerParams(vmem_limit_bytes=16 << 20),
        name="sum_parts",
    )(parts)


def per_device(query_rows, row_values, row_slots, row_counts):
    z_size = lax.axis_size("z")
    owners = HALVES * z_size
    doc_count = query_rows.shape[1]
    span = doc_count // owners
    _, _, _, cap, width = row_values.shape
    blocks = 8
    y = lax.axis_index("y")
    me = y * z_size + lax.axis_index("z")

    slots = row_slots[0, 0]
    counts = row_counts[0, 0]
    sent = payload(counts, (me * span).reshape(1), slots, row_values[0, 0], blocks=blocks)
    rows = lax.all_to_all(sent, "z", split_axis=0, concat_axis=0, tiled=True)

    half_docs = doc_count // HALVES
    mine = lax.dynamic_slice_in_dim(query_rows, y * half_docs, half_docs, 1)
    theirs = lax.dynamic_slice_in_dim(query_rows, (1 - y) * half_docs, half_docs, 1)
    mirror = lax.ppermute(theirs, "y", [(0, 1), (1, 0)])
    queries = lax.all_gather(jnp.concatenate([mine, mirror], axis=0), "z", axis=0, tiled=True)

    live = jnp.arange(cap, dtype=jnp.int32)[None, :] < counts[:, None]
    doc = slots // blocks - me * span
    beyond = jnp.maximum(counts - SHALLOW, 0)
    order = jnp.arange(owners, dtype=jnp.int32)
    before = jnp.sum(jnp.where(order[None, :] < order[:, None], beyond[None, :], 0), axis=1)
    depth = cap - SHALLOW
    spot = jnp.where(live[:, SHALLOW:], before[:, None] + jnp.arange(depth, dtype=jnp.int32)[None, :], EXTRA)
    spot = spot.reshape(1, owners * depth)
    taken = spot == jnp.arange(EXTRA, dtype=jnp.int32)[:, None]
    deep = row_values[0, 0, :, SHALLOW:, :].reshape(owners * depth, width)
    deep = jnp.dot(taken.astype(jnp.bfloat16), deep, preferred_element_type=jnp.float32).astype(jnp.bfloat16)
    packed = 1 + doc * blocks + slots % blocks + order[:, None] * (span * blocks)
    packed = jnp.sum(jnp.where(taken, packed[:, SHALLOW:].reshape(1, owners * depth), 0), axis=1)
    code = jnp.maximum(packed - 1, 0)
    target = jnp.where(packed > 0, code // (span * blocks), DEAD)
    far = jnp.stack([code % (span * blocks) // blocks, code % blocks, target]).astype(jnp.bfloat16)
    far = jnp.pad(far, ((0, 16 - 3), (SHALLOW, LANES - SHALLOW - EXTRA)))
    beside = jnp.concatenate([deep[g : g + 16] for g in range(0, EXTRA, 16)] + [far], axis=1)
    downward = [list(range(z_size - 1, -1, -1))]
    beside = lax.all_gather(beside, "z", axis=0, tiled=True, axis_index_groups=downward)
    home = jnp.stack([y, lax.axis_index("z"), jnp.int32(z_size), lax.axis_index("core")]).astype(jnp.int32)

    def lean(place, queries, beside, rows, row_values):
        return lean_tiles(place, queries, beside, rows, cap=SHALLOW, span=span, blocks=blocks, extra=EXTRA)

    def full(place, queries, beside, rows, row_values):
        block = jnp.where(live, slots % blocks, DEAD)
        meta = jnp.concatenate([doc, block], axis=1).reshape(HALVES, z_size, 2 * cap).transpose(1, 0, 2)
        meta = jnp.pad(meta, ((0, 0), (0, TILE - HALVES), (0, 0))).astype(jnp.bfloat16)
        values = row_values[0, 0]
        sent = jnp.concatenate([values[:z_size], values[z_size:], meta], axis=1)
        rows = lax.all_to_all(sent, "z", split_axis=0, concat_axis=0, tiled=True)
        return partial_tiles(place, queries, rows, cap=cap, span=span, blocks=blocks)

    flags = rows[:, HALVES * SHALLOW + TILE - 1, 0].astype(jnp.float32)
    keep, give = lax.cond(jnp.max(flags) > 0.5, full, lean, home, queries, beside, rows, row_values)
    got = lax.ppermute(give, "core", [(0, 1), (1, 0)])
    coded = merged(keep, got, blocks=blocks)
    parts = lax.all_to_all(coded, ("chip", "y"), split_axis=0, concat_axis=0, tiled=True)
    return summed(parts, blocks=blocks, width=width)


def solution(mesh):
    docs, owners = mesh.devices.shape
    shape = (docs // CORES, CORES, HALVES, owners // HALVES)
    split = Mesh(mesh.devices.reshape(shape), ("chip", "core", "y", "z"))
    doc, blk = ("chip", "core"), ("y", "z")
    in_specs = (
        P(blk, doc),
        P(doc, blk, None, None, None),
        P(doc, blk, None, None),
        P(doc, blk, None),
    )
    return jax.shard_map(
        per_device, mesh=split, in_specs=in_specs, out_specs=P(doc, blk), check_vma=False
    )
```

```python
import functools

import jax
import jax.numpy as jnp
from jax import lax
from jax.experimental import pallas as pl
from jax.experimental.pallas import tpu as pltpu
from jax.sharding import Mesh
from jax.sharding import PartitionSpec as P

CORES = 2
HALVES = 2
CODE_STEP = 64.0
TOP = 32700.0
TINY = 2.0**-110
LANES = 128
TILE = 8
SHALLOW = 96
EXTRA = 32
DEAD = 64


def coded_rows(tiles, blocks):
    lane = lax.broadcasted_iota(jnp.int32, (16, LANES), 1)
    peaks = jnp.full((16, LANES), TINY, jnp.float32)
    for b in range(blocks):
        peak = jnp.max(jnp.abs(tiles(b)), axis=1, keepdims=True)
        peaks = jnp.where(lane == b, jnp.maximum(peak, TINY), peaks)
    code = jnp.ceil((jnp.log2(peaks) - jnp.log2(TOP)) * CODE_STEP)
    inverse = jnp.exp2(code * (-1.0 / CODE_STEP))
    out = [jnp.floor(tiles(b) * inverse[:, b : b + 1] + 0.5).astype(jnp.int32).astype(jnp.int16) for b in range(blocks)]
    return out, code.astype(jnp.int32).astype(jnp.int16)


def code_tiles(place_ref, acc, keep_ref, give_ref, *, nq, blocks):
    width = acc.shape[2]
    flip, core = place_ref[0], place_ref[3]
    half = nq // (2 * 16)

    def tile_of(owner, b, m, slot):
        base = pl.multiple_of(b * nq + m * 32 + slot * 8, 8)
        return jnp.concatenate([acc[owner, pl.ds(base, 8), :], acc[owner, pl.ds(base + 16, 8), :]], axis=0)

    for owner in range(HALVES):
        for pair in range(half // CORES):
            for slot in range(2):
                target = ((slot + flip - 2 * slot * flip) * (half // CORES) + pair) * HALVES + owner
                for b in range(blocks):
                    keep_ref[target, :, b * width : (b + 1) * width] = tile_of(owner, b, pair * CORES + core, slot)
                other = lambda b: tile_of(owner, b, pair * CORES + 1 - core, slot)
                out, code = coded_rows(other, blocks)
                for b in range(blocks):
                    give_ref[target, :, b * width : (b + 1) * width] = out[b]
                give_ref[target, :, blocks * width :] = code


def merge_kernel(keep_ref, got_ref, o_ref, *, blocks):
    width = keep_ref.shape[2] // blocks
    for t in range(keep_ref.shape[0]):
        scale = jnp.exp2(got_ref[t, :, blocks * width :].astype(jnp.float32) * (1.0 / CODE_STEP))

        def total(b):
            lanes = slice(b * width, (b + 1) * width)
            return keep_ref[t, :, lanes] + got_ref[t, :, lanes].astype(jnp.float32) * scale[:, b : b + 1]

        sums = [total(b) for b in range(blocks)]
        out, code = coded_rows(lambda b: sums[b], blocks)
        for b in range(blocks):
            o_ref[t, :, b * width : (b + 1) * width] = out[b]
        o_ref[t, :, blocks * width :] = code


def merged(keep, got, *, blocks, per_step=4):
    targets, rows, lanes = got.shape
    return pl.pallas_call(
        functools.partial(merge_kernel, blocks=blocks),
        grid=(targets // per_step,),
        in_specs=[
            pl.BlockSpec((per_step, rows, keep.shape[2]), lambda i: (i, 0, 0)),
            pl.BlockSpec((per_step, rows, lanes), lambda i: (i, 0, 0)),
        ],
        out_specs=pl.BlockSpec((per_step, rows, lanes), lambda i: (i, 0, 0)),
        out_shape=jax.ShapeDtypeStruct(got.shape, jnp.int16),
        compiler_params=pltpu.CompilerParams(vmem_limit_bytes=16 << 20),
        name="merge",
    )(keep, got)


def lean_kernel(place_ref, q_ref, deep_ref, far_ref, x_ref, keep_ref, give_ref, left, acc, right_ref, *, cap, span, per_step, blocks, extra):
    step = pl.program_id(0)
    width = x_ref.shape[2]
    nq = q_ref.shape[0]
    base = HALVES * cap
    window = 2 * LANES
    tall = blocks * nq
    lane = lax.broadcasted_iota(jnp.int32, (1, LANES), 1)

    @pl.when(step == 0)
    def _():
        acc[...] = jnp.zeros_like(acc)

    places = lax.broadcasted_iota(jnp.int32, (window, window), 0)
    got, codes_of = [], []
    for k in range(per_step):
        meta = x_ref[k, base : base + TILE, :].astype(jnp.float32)
        behind = (per_step - 1 - k) * 16
        far = far_ref[behind : behind + TILE, :].astype(jnp.float32)
        docs, ids = [], []
        for owner in range(HALVES):
            lanes = slice(owner * LANES, (owner + 1) * LANES)
            to_owner = far[2:3, :] == (place_ref[1] + owner * place_ref[2]).astype(jnp.float32)
            docs.append(jnp.where(lane < cap, meta[0:1, lanes], far[0:1, :]))
            ids.append(jnp.where(lane < cap, meta[1:2, lanes], jnp.where(to_owner, far[1:2, :], float(DEAD))))
        start = k * span // LANES * LANES
        doc = jnp.concatenate(docs, axis=1).astype(jnp.int32) + (k * span - start)
        chosen = jnp.where(places == doc, 1.0, 0.0).astype(jnp.bfloat16)
        queries = q_ref[:, start : start + window]
        picked = jnp.dot(queries, chosen, preferred_element_type=jnp.float32).astype(jnp.bfloat16)
        got.append(picked)
        codes_of.append(ids)
    for owner in range(HALVES):
        lanes = slice(owner * LANES, (owner + 1) * LANES)
        for k in range(per_step):
            for b in range(blocks):
                kept = got[k][:, lanes] * jnp.where(codes_of[k][owner] == float(b), 1.0, 0.0).astype(jnp.bfloat16)
                left[owner * tall + b * nq : owner * tall + (b + 1) * nq, k * LANES : (k + 1) * LANES] = kept
        right = []
        for k in range(per_step):
            right.append(x_ref[k, owner * cap : (owner + 1) * cap, :])
            behind = (per_step - 1 - k) * 16
            right += [deep_ref[behind : behind + 16, g * width : (g + 1) * width] for g in range(extra // 16)]
        right = jnp.concatenate(right, axis=0)
        right_ref[...] = right
        acc[owner] += jnp.dot(left[owner * tall : (owner + 1) * tall, :], right_ref[...], preferred_element_type=jnp.float32)

    @pl.when(step == pl.num_programs(0) - 1)
    def _():
        code_tiles(place_ref, acc, keep_ref, give_ref, nq=nq, blocks=blocks)


def lean_tiles(place, queries, beside, rows, *, cap, span, blocks, extra, per_step=4):
    nq = queries.shape[0]
    sources, depth, width = rows.shape
    lanes = blocks * width + LANES
    targets = 16 // CORES * HALVES
    deep_lanes = extra // 16 * width
    steps = sources // per_step
    far_at = deep_lanes // LANES
    grid_spec = pltpu.PrefetchScalarGridSpec(
        num_scalar_prefetch=1,
        grid=(sources // per_step,),
        in_specs=[
            pl.BlockSpec((nq, per_step * span), lambda i, _: (0, i)),
            pl.BlockSpec((per_step * 16, deep_lanes), lambda i, _: (steps - 1 - i, 0)),
            pl.BlockSpec((per_step * 16, LANES), lambda i, _: (steps - 1 - i, far_at)),
            pl.BlockSpec((per_step, depth, width), lambda i, _: (i, 0, 0)),
        ],
        out_specs=[
            pl.BlockSpec((targets, nq // 16, blocks * width), lambda i, _: (0, 0, 0)),
            pl.BlockSpec((targets, nq // 16, lanes), lambda i, _: (0, 0, 0)),
        ],
        scratch_shapes=[
            pltpu.VMEM((HALVES * blocks * nq, per_step * (cap + extra)), jnp.bfloat16),
            pltpu.VMEM((HALVES, blocks * nq, width), jnp.float32),
            pltpu.VMEM((per_step * (cap + extra), width), jnp.bfloat16),
        ],
    )
    return pl.pallas_call(
        functools.partial(lean_kernel, cap=cap, span=span, per_step=per_step, blocks=blocks, extra=extra),
        grid_spec=grid_spec,
        out_shape=[
            jax.ShapeDtypeStruct((targets, nq // 16, blocks * width), jnp.float32),
            jax.ShapeDtypeStruct((targets, nq // 16, lanes), jnp.int16),
        ],
        compiler_params=pltpu.CompilerParams(vmem_limit_bytes=56 << 20),
        cost_estimate=pl.CostEstimate(
            flops=2 * nq * sources * HALVES * (cap + extra) * width * blocks,
            bytes_accessed=2 * (queries.size + rows.size),
            transcendentals=0,
        ),
        name="lean_tiles",
    )(place, queries, beside, beside, rows)


def gram_kernel(place_ref, q_ref, x_ref, keep_ref, give_ref, left, acc, *, cap, span, per_step, blocks):
    step = pl.program_id(0)
    width = x_ref.shape[2]
    nq = q_ref.shape[0]
    pair_rows = 2 * cap
    for owner in range(HALVES):
        for pair in range(per_step // 2):
            docs, ids = [], []
            for k in range(2):
                base = HALVES * cap
                meta = x_ref[2 * pair + k, base : base + TILE, :][owner : owner + 1, :].astype(jnp.float32)
                docs.append(meta[:, :cap] + float(k * span))
                ids.append(meta[:, cap : 2 * cap])
            doc = jnp.concatenate(docs, axis=1).astype(jnp.int32)
            block = jnp.concatenate(ids, axis=1)
            rows = lax.broadcasted_iota(jnp.int32, (2 * span, pair_rows), 0)
            chosen = jnp.where(rows == doc, 1.0, 0.0).astype(jnp.bfloat16)
            queries = q_ref[:, pair * 2 * span : (pair + 1) * 2 * span]
            picked = jnp.dot(queries, chosen, preferred_element_type=jnp.float32).astype(jnp.bfloat16)
            for b in range(blocks):
                kept = picked * jnp.where(block == float(b), 1.0, 0.0).astype(jnp.bfloat16)
                left[owner, b * nq : (b + 1) * nq, pair * pair_rows : (pair + 1) * pair_rows] = kept
        right = jnp.concatenate([x_ref[k, owner * cap : (owner + 1) * cap, :] for k in range(per_step)], axis=0)
        product = jnp.dot(left[owner], right, preferred_element_type=jnp.float32)

        @pl.when(step == 0)
        def _():
            acc[owner] = product

        @pl.when(step > 0)
        def _():
            acc[owner] += product

    @pl.when(step == pl.num_programs(0) - 1)
    def _():
        code_tiles(place_ref, acc, keep_ref, give_ref, nq=nq, blocks=blocks)


def partial_tiles(flip, queries, rows, *, cap, span, blocks, per_step=4):
    nq, docs = queries.shape
    sources, depth, width = rows.shape
    lanes = blocks * width + LANES
    targets = 16 // CORES * HALVES
    grid_spec = pltpu.PrefetchScalarGridSpec(
        num_scalar_prefetch=1,
        grid=(sources // per_step,),
        in_specs=[
            pl.BlockSpec((nq, per_step * span), lambda i, _: (0, i)),
            pl.BlockSpec((per_step, depth, width), lambda i, _: (i, 0, 0)),
        ],
        out_specs=[
            pl.BlockSpec((targets, nq // 16, blocks * width), lambda i, _: (0, 0, 0)),
            pl.BlockSpec((targets, nq // 16, lanes), lambda i, _: (0, 0, 0)),
        ],
        scratch_shapes=[
            pltpu.VMEM((HALVES, blocks * nq, per_step * cap), jnp.bfloat16),
            pltpu.VMEM((HALVES, blocks * nq, width), jnp.float32),
        ],
    )
    return pl.pallas_call(
        functools.partial(gram_kernel, cap=cap, span=span, per_step=per_step, blocks=blocks),
        grid_spec=grid_spec,
        out_shape=[
            jax.ShapeDtypeStruct((targets, nq // 16, blocks * width), jnp.float32),
            jax.ShapeDtypeStruct((targets, nq // 16, lanes), jnp.int16),
        ],
        compiler_params=pltpu.CompilerParams(vmem_limit_bytes=48 << 20),
        cost_estimate=pl.CostEstimate(
            flops=2 * nq * sources * HALVES * cap * width * blocks,
            bytes_accessed=2 * (queries.size + rows.size),
            transcendentals=0,
        ),
        name="gram_tiles",
    )(flip, queries, rows)


def payload_kernel(counts_ref, first_ref, slots_ref, low_ref, high_ref, o_ref, *, shallow, blocks):
    step = pl.program_id(0)
    here, z_size = low_ref.shape[0], low_ref.shape[0] * pl.num_programs(0)
    lane = lax.broadcasted_iota(jnp.int32, (1, slots_ref.shape[1]), 1)
    base = HALVES * shallow
    for r in range(here):
        z = step * here + r
        docs, ids = [], []
        for half in range(HALVES):
            owner = half * z_size + z
            slots = slots_ref[pl.ds(owner, 1), :]
            doc = lax.shift_right_logical(slots, blocks.bit_length() - 1) - first_ref[0]
            docs.append(doc.astype(jnp.float32))
            ids.append(jnp.where(lane < counts_ref[owner], slots & (blocks - 1), DEAD).astype(jnp.float32))
        rest = jnp.zeros((TILE - 2, o_ref.shape[2]), jnp.float32)
        meta = jnp.concatenate([jnp.concatenate(docs, axis=1), jnp.concatenate(ids, axis=1), rest], axis=0)
        o_ref[r, :shallow, :] = low_ref[r, :shallow, :]
        o_ref[r, shallow:base, :] = high_ref[r, :shallow, :]
        o_ref[r, base:, :] = meta.astype(jnp.bfloat16)


def payload(counts, first, slots, values, *, blocks, per_step=8):
    owners, cap, width = values.shape
    z_size = owners // HALVES
    depth = HALVES * SHALLOW + TILE
    steps = z_size // per_step
    grid_spec = pltpu.PrefetchScalarGridSpec(
        num_scalar_prefetch=2,
        grid=(steps,),
        in_specs=[
            pl.BlockSpec(slots.shape, lambda i, *_: (0, 0)),
            pl.BlockSpec((per_step, SHALLOW, width), lambda i, *_: (i, 0, 0)),
            pl.BlockSpec((per_step, SHALLOW, width), lambda i, *_: (i + steps, 0, 0)),
        ],
        out_specs=pl.BlockSpec((per_step, depth, width), lambda i, *_: (i, 0, 0)),
    )
    return pl.pallas_call(
        functools.partial(payload_kernel, shallow=SHALLOW, blocks=blocks),
        grid_spec=grid_spec,
        out_shape=jax.ShapeDtypeStruct((z_size, depth, width), jnp.bfloat16),
        compiler_params=pltpu.CompilerParams(vmem_limit_bytes=16 << 20),
        cost_estimate=pl.CostEstimate(flops=0, bytes_accessed=4 * values.size, transcendentals=0),
        name="payload",
    )(counts, first, slots, values, values)


def sum_kernel(p_ref, o_ref, *, blocks, width):
    groups = p_ref.shape[0]
    scale = jnp.exp2(p_ref[:, :, blocks * width :].astype(jnp.float32) * (1.0 / CODE_STEP))
    for b in range(blocks):
        total = jnp.zeros((p_ref.shape[1], width), jnp.float32)
        for g in range(groups):
            part = p_ref[g, :, b * width : (b + 1) * width].astype(jnp.float32)
            total = total + part * scale[g, :, b : b + 1]
        o_ref[:, b * width : (b + 1) * width] = total


def summed(parts, *, blocks, width):
    return pl.pallas_call(
        functools.partial(sum_kernel, blocks=blocks, width=width),
        out_shape=jax.ShapeDtypeStruct((parts.shape[1], blocks * width), jnp.float32),
        in_specs=[pl.BlockSpec(memory_space=pltpu.VMEM)],
        out_specs=pl.BlockSpec(memory_space=pltpu.VMEM),
        compiler_params=pltpu.CompilerParams(vmem_limit_bytes=16 << 20),
        name="sum_parts",
    )(parts)


def per_device(query_rows, row_values, row_slots, row_counts):
    z_size = lax.axis_size("z")
    owners = HALVES * z_size
    doc_count = query_rows.shape[1]
    span = doc_count // owners
    _, _, _, cap, width = row_values.shape
    blocks = 8
    y = lax.axis_index("y")
    me = y * z_size + lax.axis_index("z")

    slots = row_slots[0, 0]
    counts = row_counts[0, 0]
    sent = payload(counts, (me * span).reshape(1), slots, row_values[0, 0], blocks=blocks)
    rows = lax.all_to_all(sent, "z", split_axis=0, concat_axis=0, tiled=True)

    half_docs = doc_count // HALVES
    mine = lax.dynamic_slice_in_dim(query_rows, y * half_docs, half_docs, 1)
    theirs = lax.dynamic_slice_in_dim(query_rows, (1 - y) * half_docs, half_docs, 1)
    mirror = lax.ppermute(theirs, "y", [(0, 1), (1, 0)])
    queries = lax.all_gather(jnp.concatenate([mine, mirror], axis=0), "z", axis=0, tiled=True)

    live = jnp.arange(cap, dtype=jnp.int32)[None, :] < counts[:, None]
    doc = slots // blocks - me * span
    beyond = jnp.maximum(counts - SHALLOW, 0)
    order = jnp.arange(owners, dtype=jnp.int32)
    before = jnp.sum(jnp.where(order[None, :] < order[:, None], beyond[None, :], 0), axis=1)
    depth = cap - SHALLOW
    spot = jnp.where(live[:, SHALLOW:], before[:, None] + jnp.arange(depth, dtype=jnp.int32)[None, :], EXTRA)
    spot = spot.reshape(1, owners * depth)
    taken = spot == jnp.arange(EXTRA, dtype=jnp.int32)[:, None]
    deep = row_values[0, 0, :, SHALLOW:, :].reshape(owners * depth, width)
    deep = jnp.dot(taken.astype(jnp.bfloat16), deep, preferred_element_type=jnp.float32).astype(jnp.bfloat16)
    packed = 1 + doc * blocks + slots % blocks + order[:, None] * (span * blocks)
    packed = jnp.sum(jnp.where(taken, packed[:, SHALLOW:].reshape(1, owners * depth), 0), axis=1)
    code = jnp.maximum(packed - 1, 0)
    target = jnp.where(packed > 0, code // (span * blocks), DEAD)
    crowded = jnp.broadcast_to((jnp.sum(beyond) > EXTRA).astype(jnp.int32), (EXTRA,))
    far = jnp.stack([code % (span * blocks) // blocks, code % blocks, target, crowded]).astype(jnp.bfloat16)
    far = jnp.pad(far, ((0, 16 - 4), (SHALLOW, LANES - SHALLOW - EXTRA)))
    beside = jnp.concatenate([deep[g : g + 16] for g in range(0, EXTRA, 16)] + [far], axis=1)
    downward = [list(range(z_size - 1, -1, -1))]
    beside = lax.all_gather(beside, "z", axis=0, tiled=True, axis_index_groups=downward)
    home = jnp.stack([y, lax.axis_index("z"), jnp.int32(z_size), lax.axis_index("core")]).astype(jnp.int32)

    def lean(place, queries, beside, rows, row_values):
        return lean_tiles(place, queries, beside, rows, cap=SHALLOW, span=span, blocks=blocks, extra=EXTRA)

    def full(place, queries, beside, rows, row_values):
        block = jnp.where(live, slots % blocks, DEAD)
        meta = jnp.concatenate([doc, block], axis=1).reshape(HALVES, z_size, 2 * cap).transpose(1, 0, 2)
        meta = jnp.pad(meta, ((0, 0), (0, TILE - HALVES), (0, 0))).astype(jnp.bfloat16)
        values = row_values[0, 0]
        sent = jnp.concatenate([values[:z_size], values[z_size:], meta], axis=1)
        rows = lax.all_to_all(sent, "z", split_axis=0, concat_axis=0, tiled=True)
        return partial_tiles(place, queries, rows, cap=cap, span=span, blocks=blocks)

    flags = beside[:, -LANES:].reshape(z_size, 16, LANES)[:, 3, SHALLOW].astype(jnp.float32)
    keep, give = lax.cond(jnp.max(flags) > 0.5, full, lean, home, queries, beside, rows, row_values)
    got = lax.ppermute(give, "core", [(0, 1), (1, 0)])
    coded = merged(keep, got, blocks=blocks)
    parts = lax.all_to_all(coded, ("chip", "y"), split_axis=0, concat_axis=0, tiled=True)
    return summed(parts, blocks=blocks, width=width)


def solution(mesh):
    docs, owners = mesh.devices.shape
    shape = (docs // CORES, CORES, HALVES, owners // HALVES)
    split = Mesh(mesh.devices.reshape(shape), ("chip", "core", "y", "z"))
    doc, blk = ("chip", "core"), ("y", "z")
    in_specs = (
        P(blk, doc),
        P(doc, blk, None, None, None),
        P(doc, blk, None, None),
        P(doc, blk, None),
    )
    return jax.shard_map(
        per_device, mesh=split, in_specs=in_specs, out_specs=P(doc, blk), check_vma=False
    )
```
